256 devices in a mesh: chan: 32 (over y, x, core), head: 4 (over z_lo), region: 2 (over z_hi).
Axes of the slice: x: 4, y: 4, z: 8 (z_hi: 2, z_lo: 4; z = z_hi * 4 + z_lo), core: 2. Of those that a mesh axis runs over, the one named last changes fastest.
Arguments:
- tokens: bfloat16 [512, 16, 4096], P('chan', 'region', 'head'), parts along dimension 1, may hold values from -56 to 56
- position: bfloat16 [512, 4096], P('chan', 'head'), may hold values from -3 to 3
- gain: bfloat16 [4096], P('head'), may hold values from 0.099609375 to 1.8984375
- qkv_weight: bfloat16 [3, 4096, 2048], P(None, 'chan', 'head'), may hold values from -0.09375 to 0.09375
- out_weight: bfloat16 [2048, 4096], P('head'), may hold values from -0.25 to 0.25
- cotangent: bfloat16 [512, 16, 4096], P('chan', 'region', 'head'), parts along dimension 1, may hold values from -6 to 6
Outputs:
- layer_out: bfloat16 [512, 16, 4096], P('chan', 'region', 'head'), parts along dimension 1
- input_grad: bfloat16 [512, 16, 4096], P('chan', 'region', 'head'), parts along dimension 1
The draws below stay inside these ranges and needn't reach their ends.
There are 2 independent parts, one for each index of `region`. The reference program is written for one: setup_inputs(seed, part) draws one part's arguments, and reference() takes and returns one part's arrays. A program takes and returns all parts, laid end to end along the dimension named above; an argument that names none is the same for every part. Nothing has to cross between parts.
All inputs are finite; a program needn't handle non-finite values.
Results may differ from the reference program's by a relative error of at most 0.01.
Values may be sent and summed in bfloat16 or wider, within the bound.
No kernel may reach another device: no remote copies, remote signals or barrier semaphores. Data moves between devices by JAX's collectives and lax.ppermute only.
A program may use at most 64 MiB of HBM per device.

```python
import math
import jax
import jax.numpy as jnp
from jax import lax

D = 4096
HEADS_W = 16
HDIM = 128
CHG = 16
PATCH = 8
HF = 2048
CHANNELS = 512
N_CHAN = 32


def draw_tokens(key, part):
    key_pattern, key_columns, key_rows = jax.random.split(key, 3)
    array_shape = (CHANNELS, PATCH, D)
    column_frac = jnp.arange(D, dtype=jnp.float32) / D
    rising = jnp.exp(math.log(3.0) * (column_frac - 0.5))
    pattern = jnp.clip(jax.random.normal(key_pattern, array_shape, jnp.float32), -4.0, 4.0)
    columns = jnp.exp(jax.random.uniform(key_columns, (D,), jnp.float32, math.log(0.3), math.log(3.0)))
    row_scale = jnp.exp(jax.random.uniform(key_rows, (CHANNELS, PATCH, 1), jnp.float32, math.log(0.5), math.log(2.0)))
    return (pattern * columns * rising * row_scale).astype(jnp.bfloat16)


def shard_levels(key, extent, cuts, low, largest):
    def one(dim, shards_of):
        heights = jax.random.uniform(jax.random.fold_in(jax.random.fold_in(key, 6), dim), (shards_of,), jnp.float32, low / len(cuts), largest / len(cuts))
        return jnp.repeat(jnp.exp(heights), extent[dim] // shards_of).reshape((-1,) + (1,) * (len(extent) - dim - 1))

    factor_of = one(*cuts[0])
    for cut in cuts[1:]:
        factor_of = factor_of * one(*cut)
    return factor_of


def normal_values(key, extent, spread, bound, pieces=(), kind=jnp.bfloat16):
    level = shard_levels(key, extent, pieces, -0.22, 0.18) if pieces else 1.0
    drawn = jax.random.normal(key, extent, jnp.float32) * spread * level
    return jnp.minimum(jnp.maximum(drawn, -bound), bound).astype(kind)


def setup_inputs(seed: int = 0, part: int = 0) -> dict:
    seeds = jax.random.split(jax.random.key(seed), 7)
    part_keys = jax.random.split(jax.random.fold_in(seeds[6], part), 7)
    return {
        "tokens": draw_tokens(jax.random.fold_in(jax.random.fold_in(seeds[6], part), 71), part),
        "position": normal_values(seeds[1], (CHANNELS, D), 0.5, 3.0, ((0, 32), (1, 4))),
        "gain": jnp.clip(1.0 + 0.18 * jax.random.normal(seeds[2], (D,), jnp.float32), 0.099609375, 1.8984375).astype(jnp.bfloat16),
        "qkv_weight": normal_values(seeds[3], (3, D, HF), D ** -0.5, 0.09375, ((1, 32), (2, 4))),
        "out_weight": normal_values(seeds[4], (HF, D), (HF // 4) ** -0.5, 0.25, ((0, 4),)),
        "cotangent": normal_values(part_keys[5], (CHANNELS, PATCH, D), 1.0, 6.0, ((0, 32), (2, 4))),
    }


def head_norm(values):
    return values * lax.rsqrt(lax.optimization_barrier(jnp.mean(values * values, axis=-1, keepdims=True)) + 1e-06)

def within_group(queries, keys_in, values):
    factor = queries.shape[-1] ** (-0.5)
    scores = jnp.einsum('cpne,dpne->pncd', head_norm(queries), head_norm(keys_in)) * factor
    weights = jnp.exp(scores)
    weights = weights / lax.optimization_barrier(jnp.sum(weights, axis=-1, keepdims=True))
    return jnp.einsum('pncd,dpne->cpne', weights, values)

def across_groups(queries, aggregates):
    factor = queries.shape[-1] ** (-0.5)
    scores = jnp.einsum('cpne,gpne->cpng', head_norm(queries), head_norm(aggregates)) * factor
    weights = jnp.exp(scores)
    weights = weights / lax.optimization_barrier(jnp.sum(weights, axis=-1, keepdims=True))
    return jnp.einsum('cpng,gpne->cpne', weights, aggregates)

def reference(tokens, position, gain, qkv_weight, out_weight, cotangent):
    groups = N_CHAN
    channels, patches, width = tokens.shape
    row_count = channels * patches
    hidden_in = (tokens.astype(jnp.float32) + position[:, None, :].astype(jnp.float32)).astype(jnp.bfloat16)
    hidden_f = hidden_in.astype(jnp.float32)
    inv_rms = lax.rsqrt(lax.optimization_barrier(jnp.mean(hidden_f * hidden_f, axis=-1, keepdims=True)) + 1e-05)
    gain_f = gain.astype(jnp.float32)
    normed = (hidden_f * inv_rms * gain_f).astype(jnp.bfloat16).reshape(row_count, width)
    projected = []
    for index in range(3):
        product = jnp.dot(normed, qkv_weight[index], preferred_element_type=jnp.float32)
        product = lax.optimization_barrier(product.astype(jnp.bfloat16)).astype(jnp.float32)
        projected.append(product.reshape(groups, CHG, patches, HEADS_W, HDIM))
    queries, keys_in, values = projected
    first = jax.vmap(within_group)(queries, keys_in, values)
    aggregates = lax.optimization_barrier(jnp.mean(first, axis=1))
    aggregates = lax.optimization_barrier(aggregates.astype(jnp.bfloat16)).astype(jnp.float32)
    queries_flat = queries.reshape(channels, patches, HEADS_W, HDIM)
    second = across_groups(queries_flat, aggregates)
    mixed = (first.reshape(channels, patches, HEADS_W, HDIM) + second).astype(jnp.bfloat16).reshape(row_count, HF)
    branch_out = jnp.dot(mixed, out_weight, preferred_element_type=jnp.float32).reshape(channels, patches, width)
    layer_out = (hidden_f + branch_out).astype(jnp.bfloat16)
    grad_mixed = lax.dot_general(cotangent.reshape(row_count, width), out_weight, (((1,), (1,)), ((), ())), preferred_element_type=jnp.float32)
    grad_mixed = grad_mixed.reshape(channels, patches, HEADS_W, HDIM)
    unused_second, back_across = jax.vjp(across_groups, queries_flat, aggregates)
    grad_q_second, grad_aggregates = back_across(grad_mixed)
    grad_first = grad_mixed.reshape(groups, CHG, patches, HEADS_W, HDIM) + grad_aggregates[:, None] / CHG
    unused_first, back_within = jax.vjp(jax.vmap(within_group), queries, keys_in, values)
    grad_q, grad_k, grad_v = back_within(grad_first)
    grad_q = grad_q.reshape(channels, patches, HEADS_W, HDIM) + grad_q_second
    rounded = [grad_q.astype(jnp.bfloat16), grad_k.astype(jnp.bfloat16), grad_v.astype(jnp.bfloat16)]
    grad_normed = jnp.zeros((row_count, width), jnp.float32)
    for index in range(3):
        grad_normed = grad_normed + lax.dot_general(rounded[index].reshape(row_count, HF), qkv_weight[index], (((1,), (1,)), ((), ())), preferred_element_type=jnp.float32)
    grad_normed = grad_normed.reshape(channels, patches, width)
    correction = lax.optimization_barrier(jnp.mean(hidden_f * gain_f * grad_normed, axis=-1, keepdims=True))
    grad_hidden = inv_rms * gain_f * grad_normed - hidden_f * inv_rms * inv_rms * inv_rms * correction
    input_grad = (cotangent.astype(jnp.float32) + grad_hidden).astype(jnp.bfloat16)
    return (layer_out, input_grad)
```

```python
import functools
import jax
import jax.numpy as jnp
from jax import lax
from jax.experimental import pallas as pl
from jax.experimental.pallas import tpu as pltpu
from jax.sharding import PartitionSpec as P

F32 = jnp.float32
BF = jnp.bfloat16
NY, NX, NC, NZ = 4, 4, 2, 4
HD = 128
FAC = HD ** -0.5
CHG = 16
PAT = 8


def chan_id(y, x, c):
    return (y % NY) * (NX * NC) + (x % NX) * NC + (c % NC)


SITES = [(y, x, c) for y in range(NY) for x in range(NX) for c in range(NC)]
SWAP = [(chan_id(y, x, c), chan_id(y, x, c + 1)) for y, x, c in SITES]
SAME_CORE = [[chan_id(y, x, c) for y in range(NY) for x in range(NX)] for c in range(NC)]


def ring(first, step):
    pairs = []
    for y, x, c in SITES:
        if (c == 0) == first:
            pairs.append((chan_id(y, x, c), chan_id(y, x + step, c)))
        else:
            pairs.append((chan_id(y, x, c), chan_id(y + step, x, c)))
    return pairs


def swap(value):
    return lax.ppermute(value, "chan", SWAP)


def zshift(value, step):
    return lax.ppermute(value, "head", [(i, (i + step) % NZ) for i in range(NZ)])


def dot_nt(a, b):
    return lax.dot_general(a, b, (((1,), (1,)), ((), ())), preferred_element_type=F32)


def dot_nn(a, b):
    return lax.dot_general(a, b, (((1,), (0,)), ((), ())), preferred_element_type=F32)


def dot_tn(a, b):
    return lax.dot_general(a, b, (((0,), (0,)), ((), ())), preferred_element_type=F32)


def inv_norm(u):
    return lax.rsqrt(jnp.mean(u * u, axis=-1, keepdims=True) + 1e-06)


def norm_back(u, r, dy):
    return r * dy - u * (r * r * r * jnp.mean(dy * u, axis=-1, keepdims=True))


def same_patch(rows, cols):
    ri = lax.broadcasted_iota(jnp.int32, (rows, cols), 0) % PAT
    ci = lax.broadcasted_iota(jnp.int32, (rows, cols), 1) % PAT
    return ri == ci


def softmax_rows(scores, mask):
    e = jnp.where(mask, jnp.exp(scores), 0.0)
    return e / jnp.sum(e, axis=-1, keepdims=True)


def project_kernel(tab, own, oth, wx, wr, wl, wro, wlo, proj, first, agg, wv, acc, sems):
    parts = ((wx, 0, 1024), (wr, 1024, 1024), (wl, 2048, 1024), (wro, 3072, 512), (wlo, 3584, 512))
    copies = []
    for n, (ref, at, size) in enumerate(parts):
        copy = pltpu.make_async_copy(ref, wv.at[pl.ds(at, size)], sems.at[n])
        copy.start()
        copies.append(copy)
    acc[...] = jnp.zeros_like(acc)
    for n, (ref, at, size) in enumerate(parts):
        copies[n].wait()
        for i in range(at // 256, (at + size) // 256):
            blk = tab[i]
            w = wv[pl.ds(i * 256, 256), :]
            acc[0:128, :] += dot_nn(own[blk], w)
            acc[128:256, :] += dot_nn(oth[blk], w)
    proj[...] = acc[...].astype(BF)
    mask = same_patch(128, 128)
    for g in range(2):
        rows = pl.ds(g * 128, 128)
        for h in range(2):
            q = proj[rows, pl.ds(h * 128, 128)]
            k = proj[rows, pl.ds(256 + h * 128, 128)]
            v = proj[rows, pl.ds(512 + h * 128, 128)]
            kf = k.astype(F32)
            kn = (kf * inv_norm(kf)).astype(BF)
            s = dot_nt(q, kn) * (inv_norm(q.astype(F32)) * FAC)
            w = softmax_rows(s, mask)
            f = dot_nn(w.astype(BF), v)
            first[rows, pl.ds(h * 128, 128)] = f
            m = jnp.sum(f.reshape(CHG, PAT, HD), axis=0) * (1.0 / CHG)
            agg[h, pl.ds(g * PAT, PAT), :] = m.astype(BF)


def across_kernel(proj, first, agg, gm, mixed, gq2, gagg):
    mask = same_patch(256, 256)
    for h in range(2):
        cols = pl.ds(h * 128, 128)
        q = proj[:, cols]
        qf = q.astype(F32)
        rq = inv_norm(qf)
        a = agg[:, h].reshape(256, HD)
        af = a.astype(F32)
        ra = inv_norm(af)
        an = (af * ra).astype(BF)
        s = dot_nt(q, an) * (rq * FAC)
        w = softmax_rows(s, mask)
        wb = w.astype(BF)
        mixed[:, cols] = (first[:, cols] + dot_nn(wb, a)).astype(BF)
        g = gm[:, cols].astype(BF)
        dw = dot_nt(g, a)
        ds = w * (dw - jnp.sum(w * dw, axis=-1, keepdims=True)) * FAC
        dsb = ds.astype(BF)
        gq2[:, cols] = norm_back(qf, rq, dot_nn(dsb, an))
        dan = dot_tn(dsb, (qf * rq).astype(BF))
        da = dot_tn(wb, g) + norm_back(af, ra, dan)
        gagg[:, h] = da.astype(BF).reshape(16, 16, HD)


def back_kernel(inv, proj, gm, gq2, ragg, wx, wr, wl, wro, wlo, out, corr, wv, stk, sems):
    parts = ((wx, 0, 1024), (wr, 1024, 1024), (wl, 2048, 1024), (wro, 3072, 512), (wlo, 3584, 512))
    copies = []
    for n, (ref, at, size) in enumerate(parts):
        copy = pltpu.make_async_copy(ref, wv.at[pl.ds(at, size)], sems.at[n])
        copy.start()
        copies.append(copy)
    own_grad = jnp.sum(ragg[...].astype(F32), axis=0) * (1.0 / CHG)
    mask = same_patch(128, 128)
    for g in range(2):
        rows = pl.ds(g * 128, 128)
        total = jnp.zeros((128, 1), F32)
        for h in range(2):
            cols = pl.ds(h * 128, 128)
            q = proj[rows, cols]
            k = proj[rows, pl.ds(256 + h * 128, 128)]
            v = proj[rows, pl.ds(512 + h * 128, 128)]
            qf = q.astype(F32)
            kf = k.astype(F32)
            rq = inv_norm(qf)
            rk = inv_norm(kf)
            kn = (kf * rk).astype(BF)
            w = softmax_rows(dot_nt(q, kn) * (rq * FAC), mask)
            og = own_grad[h, g * PAT:(g + 1) * PAT, :]
            gf = gm[rows, cols] + jnp.broadcast_to(og[None], (CHG, PAT, HD)).reshape(128, HD)
            gb = gf.astype(BF)
            dv = dot_tn(w.astype(BF), gb)
            dw = dot_nt(gb, v)
            ds = w * (dw - jnp.sum(w * dw, axis=-1, keepdims=True)) * FAC
            dsb = ds.astype(BF)
            dq = norm_back(qf, rq, dot_nn(dsb, kn)) + gq2[rows, cols]
            dk = norm_back(kf, rk, dot_tn(dsb, (qf * rq).astype(BF)))
            dq = dq.astype(BF)
            dk = dk.astype(BF)
            dv = dv.astype(BF)
            stk[rows, cols] = dq
            stk[rows, pl.ds(256 + h * 128, 128)] = dk
            stk[rows, pl.ds(512 + h * 128, 128)] = dv
            prod = dq.astype(F32) * qf + dk.astype(F32) * kf + dv.astype(F32) * v.astype(F32)
            total = total + jnp.sum(prod, axis=-1, keepdims=True)
        corr[rows, :] = jnp.broadcast_to(total, (128, 128))
    for copy in copies:
        copy.wait()
    for d in range(4):
        for x in range(4):
            i = inv[d * 4 + x]
            w = wv[pl.ds(pl.multiple_of(i * 256, 256), 256), :]
            r = dot_nt(stk[...], w)
            out[0, d, :, pl.ds(x * 256, 256)] = r[0:128].astype(BF)
            out[1, d, :, pl.ds(x * 256, 256)] = r[128:256].astype(BF)


VM = pl.BlockSpec(memory_space=pltpu.VMEM)
SM = pl.BlockSpec(memory_space=pltpu.SMEM)
AN = pl.BlockSpec(memory_space=pl.ANY)
PARAMS = pltpu.CompilerParams(vmem_limit_bytes=48 * 1024 * 1024)


def shape(dims, dtype):
    return jax.ShapeDtypeStruct(dims, dtype)


def project(tab, own, oth, weights):
    return pl.pallas_call(
        project_kernel,
        in_specs=[SM, VM, VM] + [AN] * 5,
        out_specs=[VM, VM, VM],
        out_shape=[shape((256, 768), BF), shape((256, 256), F32), shape((2, 16, HD), BF)],
        scratch_shapes=[pltpu.VMEM((4096, 768), BF), pltpu.VMEM((256, 768), F32), pltpu.SemaphoreType.DMA((5,))],
        compiler_params=PARAMS,
        name="project",
    )(tab, own, oth, *weights)


def across(proj, first, agg, gm):
    return pl.pallas_call(
        across_kernel,
        in_specs=[VM] * 4,
        out_specs=[VM] * 3,
        out_shape=[shape((256, 256), BF), shape((256, 256), F32), shape((16, 2, 16, HD), BF)],
        compiler_params=PARAMS,
        name="across",
    )(proj, first, agg, gm)


def backward(inv, proj, gm, gq2, ragg, weights):
    return pl.pallas_call(
        back_kernel,
        in_specs=[SM] + [VM] * 4 + [AN] * 5,
        out_specs=[VM, VM],
        out_shape=[shape((2, 4, 128, 1024), BF), shape((256, 128), F32)],
        scratch_shapes=[pltpu.VMEM((4096, 768), BF), pltpu.VMEM((256, 768), BF), pltpu.SemaphoreType.DMA((5,))],
        compiler_params=PARAMS,
        name="backward",
    )(inv, proj, gm, gq2, ragg, *weights)


def gather_weights(qkv_weight, core):
    wt = qkv_weight.transpose(1, 0, 2).reshape(128, 3, 2, 256)
    mine = lax.dynamic_index_in_dim(wt, core, 2, False).reshape(128, 768)
    other = lax.dynamic_index_in_dim(wt, 1 - core, 2, False).reshape(128, 768)
    got = swap(other)
    lead = core == 0
    own = jnp.concatenate([jnp.where(lead, mine, got), jnp.where(lead, got, mine)], 0)

    def phase(block, first):
        half = block.shape[0] // 2
        fwd = lax.ppermute(block, "chan", ring(first, 1))
        bwd = lax.ppermute(block, "chan", ring(first, -1))
        far_a = lax.ppermute(fwd[:half], "chan", ring(first, 1))
        far_b = lax.ppermute(bwd[half:], "chan", ring(first, -1))
        return fwd, bwd, far_a, far_b

    row = jnp.concatenate((own,) + phase(own, True), 0)
    return (row,) + phase(row, False)


OFFS = (0, 3, 1, 2)


def tables(y, x, core, z):
    lead = core == 0
    fwd = []
    for s3 in OFFS:
        for s1 in OFFS:
            by = (y + jnp.where(lead, s3, s1)) % 4
            bx = (x + jnp.where(lead, s1, s3)) % 4
            fwd.append(((z - by) % 4) * 4 + bx)
    where_of = jnp.array([0, 2, 3, 1], jnp.int32)
    back = []
    for d in range(4):
        by = (z + d) % 4
        for bx in range(4):
            py = where_of[(by - y) % 4]
            px = where_of[(bx - x) % 4]
            back.append(jnp.where(lead, py * 4 + px, px * 4 + py))
    return jnp.stack(fwd).astype(jnp.int32), jnp.stack(back).astype(jnp.int32)


def per_device(tokens, position, gain, qkv_weight, out_weight, cotangent):
    chan = lax.axis_index("chan")
    z = lax.axis_index("head")
    core = chan % 2
    x = (chan // 2) % 4
    y = chan // 8
    tab, inv = tables(y, x, core, z)
    lead = core == 0

    hidden_in = (tokens.astype(F32) + position[:, None, :].astype(F32)).astype(BF)
    hidden_in = hidden_in.reshape(128, 1024)
    message = jnp.concatenate([hidden_in, jnp.broadcast_to(gain[None], (8, 1024))], 0)
    h_parts = [message, zshift(message, 1), zshift(message, 2), zshift(message, 3)]
    weights = gather_weights(qkv_weight, core)
    cot = cotangent.reshape(128, 1024)
    c_parts = [cot, zshift(cot, 1), zshift(cot, 2), zshift(cot, 3)]

    hid = [p[:128].astype(F32) for p in h_parts]
    gains = [p[128:129].astype(F32) for p in h_parts]
    square = sum(jnp.sum(h * h, axis=-1, keepdims=True) for h in hid)
    inv_rms = lax.rsqrt(square * (1.0 / 4096) + 1e-05)
    normed = jnp.concatenate(
        [
            (h * inv_rms * g).astype(BF).reshape(128, 4, 256).transpose(1, 0, 2)
            for h, g in zip(hid, gains)
        ],
        0,
    )
    normed_other = swap(normed)
    proj, first, agg = project(tab, normed, normed_other, weights)
    agg_all = lax.all_to_all(
        jnp.broadcast_to(agg[None], (16, 2, 16, HD)), "chan", 0, 0,
        axis_index_groups=SAME_CORE, tiled=True,
    )

    gm_all = sum(
        dot_nt(c, lax.dynamic_slice_in_dim(out_weight, ((z - d) % 4) * 1024, 1024, 1))
        for d, c in enumerate(c_parts)
    )
    gm_mine = jnp.where(lead, gm_all[:, :256], gm_all[:, 256:])
    gm_other = jnp.where(lead, gm_all[:, 256:], gm_all[:, :256])
    gm = jnp.concatenate([gm_mine, swap(gm_other)], 0)

    mixed, gq2, gagg = across(proj, first, agg_all, gm)
    ragg = lax.all_to_all(gagg, "chan", 0, 0, axis_index_groups=SAME_CORE, tiled=True)

    mix_own = mixed[:128]
    mix_got = swap(mixed[128:])
    mix = jnp.concatenate([jnp.where(lead, mix_own, mix_got), jnp.where(lead, mix_got, mix_own)], 1)
    part = dot_nn(mix, out_weight)

    def quarter(value, d):
        return lax.dynamic_slice_in_dim(value, ((z + d) % 4) * 1024, 1024, 1)

    part_b = part.astype(BF)
    summed = quarter(part, 0) + sum(zshift(quarter(part_b, d), d).astype(F32) for d in (1, 2, 3))
    layer_out = (summed + hidden_in.astype(F32)).astype(BF)

    out, corr = backward(inv, proj, gm, gq2, ragg, weights)
    corr_all = (corr[:128, :1] + swap(corr[128:])[:, :1]) * (1.0 / 4096)
    got = swap(out[1])

    def partial(d):
        src = (4 - d) % 4
        gn = out[0, d].astype(F32) + got[d].astype(F32)
        return inv_rms * (gains[src] * gn - hid[src] * (inv_rms * corr_all))

    grad = partial(0) + sum(zshift(partial(d).astype(BF), d).astype(F32) for d in (1, 2, 3))
    input_grad = (cot.astype(F32) + grad).astype(BF)
    return layer_out.reshape(16, 8, 1024), input_grad.reshape(16, 8, 1024)


def solution(mesh):
    return jax.shard_map(
        per_device,
        mesh=mesh,
        in_specs=(
            P("chan", "region", "head"),
            P("chan", "head"),
            P("head"),
            P(None, "chan", "head"),
            P("head", None),
            P("chan", "region", "head"),
        ),
        out_specs=(P("chan", "region", "head"), P("chan", "region", "head")),
        check_vma=False,
    )
```

```python
import jax
import jax.numpy as jnp
from jax import lax
from jax.experimental import pallas as pl
from jax.experimental.pallas import tpu as pltpu
from jax.sharding import PartitionSpec as P


F32 = jnp.float32
BF = jnp.bfloat16
NY, NX, NC, NZ = 4, 4, 2, 4
HD = 128
FAC = HD ** -0.5
CHG = 16
PAT = 8


def chan_id(y, x, c):
    return (y % NY) * (NX * NC) + (x % NX) * NC + (c % NC)


SITES = [(y, x, c) for y in range(NY) for x in range(NX) for c in range(NC)]
SWAP = [(chan_id(y, x, c), chan_id(y, x, c + 1)) for y, x, c in SITES]
SAME_CORE = [[chan_id(y, x, c) for y in range(NY) for x in range(NX)] for c in range(NC)]


def ring(first, step):
    pairs = []
    for y, x, c in SITES:
        if (c == 0) == first:
            pairs.append((chan_id(y, x, c), chan_id(y, x + step, c)))
        else:
            pairs.append((chan_id(y, x, c), chan_id(y + step, x, c)))
    return pairs


def swap(value):
    return lax.ppermute(value, "chan", SWAP)


def zshift(value, step):
    return lax.ppermute(value, "head", [(i, (i + step) % NZ) for i in range(NZ)])


def dot_nt(a, b):
    return lax.dot_general(a, b, (((1,), (1,)), ((), ())), preferred_element_type=F32)


def dot_nn(a, b):
    return lax.dot_general(a, b, (((1,), (0,)), ((), ())), preferred_element_type=F32)


def dot_tn(a, b):
    return lax.dot_general(a, b, (((0,), (0,)), ((), ())), preferred_element_type=F32)


def inv_norm(u):
    return lax.rsqrt(jnp.mean(u * u, axis=-1, keepdims=True) + 1e-06)


def norm_back(u, r, dy):
    return r * dy - u * (r * r * r * jnp.mean(dy * u, axis=-1, keepdims=True))


def same_patch(rows, cols):
    ri = lax.broadcasted_iota(jnp.int32, (rows, cols), 0) % PAT
    ci = lax.broadcasted_iota(jnp.int32, (rows, cols), 1) % PAT
    return ri == ci


def softmax_rows(scores, mask):
    e = jnp.where(mask, jnp.exp(scores), 0.0)
    return e / jnp.sum(e, axis=-1, keepdims=True)


def place():
    chan = lax.axis_index("chan")
    return chan // 8, (chan // 2) % 4, chan % 2, lax.axis_index("head")


def slot_of(off):
    return jnp.where(off == 3, 1, jnp.where(off == 1, 2, jnp.where(off == 2, 3, 0)))


def off_of(slot):
    return jnp.where(slot == 1, 3, jnp.where(slot == 2, 1, jnp.where(slot == 3, 2, 0)))


def within(proj, rows, h, mask):
    q = proj[rows, pl.ds(h * 128, 128)]
    k = proj[rows, pl.ds(256 + h * 128, 128)]
    v = proj[rows, pl.ds(512 + h * 128, 128)]
    qf = q.astype(F32)
    kf = k.astype(F32)
    rq = inv_norm(qf)
    rk = inv_norm(kf)
    kn = (kf * rk).astype(BF)
    w = softmax_rows(dot_nt(q, kn) * (rq * FAC), mask)
    return qf, kf, v, rq, rk, kn, w


def prepare_kernel(tokens, position, gain, message):
    hidden = tokens[...].astype(F32) + position[...].astype(F32)[:, None, :]
    message[0:128, :] = hidden.reshape(128, 1024).astype(BF)
    message[128:136, :] = jnp.broadcast_to(gain[...], (8, 1024))


def norm_kernel(p0, p1, p2, p3, normed, inv):
    parts = (p0, p1, p2, p3)
    square = jnp.zeros((128, 1), F32)
    for p in parts:
        h = p[0:128, :].astype(F32)
        square = square + jnp.sum(h * h, axis=-1, keepdims=True)
    r = lax.rsqrt(square * (1.0 / 4096) + 1e-05)
    inv[...] = jnp.broadcast_to(r, (128, 128))
    for n, p in enumerate(parts):
        for b in range(4):
            cols = pl.ds(b * 256, 256)
            h = p[0:128, cols].astype(F32)
            g = p[128:136, cols].astype(F32)[0:1]
            normed[n * 4 + b] = (h * r * g).astype(BF)


PIECES = (
    (0, 1), (1, 2), (3, 1), (4, 1), (8, 1), (5, 2), (9, 2), (7, 1), (11, 1),
    (12, "a"), (12, "b"), (13, 1), (14, 1), (15, "a"), (15, "b"),
)


def project_kernel(own, oth, *refs):
    pieces = refs[:15]
    proj, agg, wall, wv, acc, sems, out_sems = refs[15:]
    copies = []
    for n, (ref, (slot, size)) in enumerate(zip(pieces, PIECES)):
        if size == "a":
            dst = wv.at[slot, 0:1]
        elif size == "b":
            dst = wv.at[slot, 1:2]
        else:
            dst = wv.at[slot:slot + size]
        copy = pltpu.make_async_copy(ref, dst, sems.at[n])
        copy.start()
        copies.append(copy)
    y, x, core, z = place()
    lead = core == 0
    acc[...] = jnp.zeros_like(acc)

    def step(i, carry):
        s3 = off_of(i // 4)
        s1 = off_of(i % 4)
        by = (y + jnp.where(lead, s3, s1)) % 4
        bx = (x + jnp.where(lead, s1, s3)) % 4
        blk = ((z + 4 - by) % 4) * 4 + bx
        lhs = jnp.concatenate([own[blk], oth[blk]], 0)
        for j in range(3):
            w = wv[i, :, j].reshape(256, 256)
            acc[:, j * 256:(j + 1) * 256] += dot_nn(lhs, w)
        return carry

    for copy in copies[:9]:
        copy.wait()
    lax.fori_loop(0, 12, step, 0)
    for copy in copies[9:]:
        copy.wait()
    back = pltpu.make_async_copy(wv, wall, out_sems.at[0])
    back.start()
    lax.fori_loop(12, 16, step, 0)
    proj[...] = acc[...].astype(BF)
    mask = same_patch(128, 128)
    for g in range(2):
        for h in range(2):
            _, _, v, _, _, _, w = within(proj, pl.ds(g * 128, 128), h, mask)
            f = dot_nn(w.astype(BF), v)
            m = jnp.sum(f.reshape(CHG, PAT, HD), axis=0) * (1.0 / CHG)
            agg[:, h, pl.ds(g * PAT, PAT), :] = jnp.broadcast_to(m.astype(BF)[None], (16, PAT, HD))
    back.wait()


def across_kernel(proj, agg, gm, mix_own, mix_oth, gg, gagg):
    mask = same_patch(256, 256)
    small = same_patch(128, 128)
    for h in range(2):
        cols = pl.ds(h * 128, 128)
        q = proj[:, cols]
        qf = q.astype(F32)
        rq = inv_norm(qf)
        a = agg[:, h].reshape(256, HD)
        af = a.astype(F32)
        ra = inv_norm(af)
        an = (af * ra).astype(BF)
        s = dot_nt(q, an) * (rq * FAC)
        w = softmax_rows(s, mask)
        wb = w.astype(BF)
        second = dot_nn(wb, a)
        for g, ref in enumerate((mix_own, mix_oth)):
            fine = within(proj, pl.ds(g * 128, 128), h, small)
            first = dot_nn(fine[6].astype(BF), fine[2])
            ref[:, cols] = (first + second[g * 128:(g + 1) * 128]).astype(BF)
        gf = gm[:, cols]
        g = gf.astype(BF)
        dw = dot_nt(g, a)
        ds = w * (dw - jnp.sum(w * dw, axis=-1, keepdims=True)) * FAC
        dsb = ds.astype(BF)
        gg[:, cols] = gf
        gg[:, pl.ds(256 + h * 128, 128)] = norm_back(qf, rq, dot_nn(dsb, an))
        dan = dot_tn(dsb, (qf * rq).astype(BF))
        da = dot_tn(wb, g) + norm_back(af, ra, dan)
        gagg[:, h] = da.astype(BF).reshape(16, 16, HD)


def quarter_slots(d):
    y, x, core, z = place()
    by = (z + d) % 4
    py = slot_of((by + 4 - y) % 4)
    slots = []
    for bx in range(4):
        px = slot_of((bx + 4 - x) % 4)
        slots.append(jnp.where(core == 0, py * 4 + px, px * 4 + py))
    return slots


def fetch(wall, wv, sems, d, at):
    copies = []
    for bx, slot in enumerate(quarter_slots(d)):
        copy = pltpu.make_async_copy(wall.at[slot], wv.at[at + bx], sems.at[at + bx])
        copy.start()
        copies.append(copy)
    return copies


def block_product(stk, wv, n):
    r = jnp.zeros((256, 256), F32)
    for j in range(3):
        r = r + dot_nt(stk[:, j * 256:(j + 1) * 256], wv[n, :, j].reshape(256, 256))
    return r


def back_kernel(proj, gg, ragg, wall, own, oth, stk, corr_own, corr_oth, wv, sems):
    copies = fetch(wall, wv, sems, 2, 0)
    own_grad = jnp.sum(ragg[...].astype(F32), axis=0) * (1.0 / CHG)
    mask = same_patch(128, 128)
    for g, ref in enumerate((corr_own, corr_oth)):
        rows = pl.ds(g * 128, 128)
        total = jnp.zeros((128, 1), F32)
        for h in range(2):
            cols = pl.ds(h * 128, 128)
            qf, kf, v, rq, rk, kn, w = within(proj, rows, h, mask)
            og = own_grad[h, g * PAT:(g + 1) * PAT, :]
            gf = gg[rows, cols] + jnp.broadcast_to(og[None], (CHG, PAT, HD)).reshape(128, HD)
            gb = gf.astype(BF)
            dv = dot_tn(w.astype(BF), gb)
            dw = dot_nt(gb, v)
            ds = w * (dw - jnp.sum(w * dw, axis=-1, keepdims=True)) * FAC
            dsb = ds.astype(BF)
            dq = norm_back(qf, rq, dot_nn(dsb, kn)) + gg[rows, pl.ds(256 + h * 128, 128)]
            dk = norm_back(kf, rk, dot_tn(dsb, (qf * rq).astype(BF)))
            dq = dq.astype(BF)
            dk = dk.astype(BF)
            dv = dv.astype(BF)
            stk[rows, cols] = dq
            stk[rows, pl.ds(256 + h * 128, 128)] = dk
            stk[rows, pl.ds(512 + h * 128, 128)] = dv
            prod = dq.astype(F32) * qf + dk.astype(F32) * kf + dv.astype(F32) * v.astype(F32)
            total = total + jnp.sum(prod, axis=-1, keepdims=True)
        ref[...] = jnp.broadcast_to(total, (128, 128))
    for copy in copies:
        copy.wait()

    def step(bx, carry):
        r = block_product(stk, wv, bx)
        cols = pl.ds(pl.multiple_of(bx * 256, 256), 256)
        own[:, cols] = r[0:128].astype(BF)
        oth[:, cols] = r[128:256].astype(BF)
        return carry

    lax.fori_loop(0, 4, step, 0)


def rest_kernel(stk, wall, own, oth, wv, sems):
    copies = []
    for n, d in enumerate((1, 3, 0)):
        copies.append(fetch(wall, wv, sems, d, n * 4))
    for n in range(3):
        for copy in copies[n]:
            copy.wait()

        def step(bx, carry):
            r = block_product(stk, wv, n * 4 + bx)
            cols = pl.ds(pl.multiple_of(bx * 256, 256), 256)
            own[n, :, cols] = r[0:128].astype(BF)
            oth[n, :, cols] = r[128:256].astype(BF)
            return carry

        lax.fori_loop(0, 4, step, 0)


def combine(mine, got, part, inv, corr_own, corr_got):
    r = inv[:, 0:1]
    c = (corr_own[:, 0:1] + corr_got[:, 0:1]) * (r * (1.0 / 4096))
    h = part[0:128, :].astype(F32)
    g = part[128:136, :].astype(F32)[0:1]
    return r * (g * (mine.astype(F32) + got.astype(F32)) - h * c)


def one_kernel(mine, got, part, inv, corr_own, corr_got, out):
    out[...] = combine(mine[...], got[...], part, inv, corr_own, corr_got).astype(BF)


def two_kernel(mine, got, part_a, part_b, inv, corr_own, corr_got, out_a, out_b):
    out_a[...] = combine(mine[0], got[0], part_a, inv, corr_own, corr_got).astype(BF)
    out_b[...] = combine(mine[1], got[1], part_b, inv, corr_own, corr_got).astype(BF)


def last_kernel(mine, got, part, inv, corr_own, corr_got, cot, r1, r2, r3, out):
    grad = combine(mine[2], got[2], part, inv, corr_own, corr_got)
    grad = grad + r1[...].astype(F32) + r2[...].astype(F32) + r3[...].astype(F32)
    out[...] = (cot[...].astype(F32) + grad).astype(BF)


VM = pl.BlockSpec(memory_space=pltpu.VMEM)
AN = pl.BlockSpec(memory_space=pl.ANY)
HB = pl.BlockSpec(memory_space=pltpu.HBM)
PARAMS = pltpu.CompilerParams(vmem_limit_bytes=16 * 1024 * 1024)


def shape(dims, dtype):
    return jax.ShapeDtypeStruct(dims, dtype)


def call(kernel, ins, outs, args, scratch=()):
    return pl.pallas_call(
        kernel,
        in_specs=ins,
        out_specs=[spec for spec, _ in outs],
        out_shape=[sh for _, sh in outs],
        scratch_shapes=list(scratch),
        compiler_params=PARAMS,
    )(*args)


BLOCK = (2, 3, 128, 256)


def prepare(tokens, position, gain):
    return call(prepare_kernel, [VM] * 3, [(VM, shape((136, 1024), BF))], (tokens, position, gain))[0]


def normalise(parts):
    return call(
        norm_kernel, [VM] * 4,
        [(VM, shape((16, 128, 256), BF)), (VM, shape((128, 128), F32))], parts,
    )


def project(own, oth, weights):
    return call(
        project_kernel, [VM, VM] + [AN] * 15,
        [(VM, shape((256, 768), BF)), (VM, shape((16, 2, 16, HD), BF)), (HB, shape((16,) + BLOCK, BF))],
        (own, oth) + weights,
        (
            pltpu.VMEM((16,) + BLOCK, BF), pltpu.VMEM((256, 768), F32),
            pltpu.SemaphoreType.DMA((15,)), pltpu.SemaphoreType.DMA((1,)),
        ),
    )


def across(proj, agg, gm):
    return call(
        across_kernel, [VM] * 3,
        [
            (VM, shape((128, 256), BF)), (VM, shape((128, 256), BF)),
            (VM, shape((256, 512), F32)), (VM, shape((16, 2, 16, HD), BF)),
        ],
        (proj, agg, gm),
    )


def backward(proj, gg, ragg, wall):
    return call(
        back_kernel, [VM] * 3 + [HB],
        [
            (VM, shape((128, 1024), BF)), (VM, shape((128, 1024), BF)), (VM, shape((256, 768), BF)),
            (VM, shape((128, 128), F32)), (VM, shape((128, 128), F32)),
        ],
        (proj, gg, ragg, wall),
        (pltpu.VMEM((4,) + BLOCK, BF), pltpu.SemaphoreType.DMA((4,))),
    )


def rest(stk, wall):
    return call(
        rest_kernel, [VM, HB],
        [(VM, shape((3, 128, 1024), BF)), (VM, shape((3, 128, 1024), BF))],
        (stk, wall),
        (pltpu.VMEM((12,) + BLOCK, BF), pltpu.SemaphoreType.DMA((12,))),
    )


def own_weights(qkv_weight, core):
    mine = lax.dynamic_slice_in_dim(qkv_weight, core * 256, 256, 2)
    other = lax.dynamic_slice_in_dim(qkv_weight, (1 - core) * 256, 256, 2)
    got = swap(other)
    lead = core == 0
    return jnp.stack([jnp.where(lead, mine, got), jnp.where(lead, got, mine)])


def gather_weights(own):
    def near(value, step):
        return lax.ppermute(value, "chan", ring(True, step))

    def cross(value, step):
        return lax.ppermute(value, "chan", ring(False, step))

    r = near(own, 1)
    l = near(own, -1)
    up = cross(own, 1)
    down = cross(own, -1)
    pair = jnp.stack([r, l])

    far = jnp.concatenate([near(r[:1], 1), near(l[1:], -1)], 0)
    pair_up = cross(pair, 1)
    pair_down = cross(pair, -1)
    over_a = cross(up[:1], 1)
    over_b = cross(down[1:], -1)
    far_up = cross(far, 1)
    far_down = cross(far, -1)
    pair_a = cross(pair_up[0], 1)
    pair_b = cross(pair_down[1], -1)
    far_a = cross(far_up[:1], 1)
    far_b = cross(far_down[1:], -1)

    def whole(value):
        return value.reshape((-1,) + value.shape[-4:])

    lead = tuple(whole(v) for v in (own, pair, far, up, down, pair_up, pair_down, far_up, far_down))
    tail = (over_a, over_b, whole(pair_a), whole(pair_b), far_a, far_b)
    return lead + tail, far


def layer(tokens, position, gain, qkv_weight, out_weight, cotangent):
    _, _, core, z = place()
    lead = core == 0

    own_w = own_weights(qkv_weight, core)
    message = prepare(tokens, position, gain.reshape(1, 1024))
    h_parts = [message] + [zshift(message, d) for d in (1, 2, 3)]
    weights, far = gather_weights(own_w)

    waited, _ = lax.optimization_barrier((h_parts, far))
    normed, inv_rms = normalise(waited)
    cot = cotangent.reshape(128, 1024)
    cot_b, normed = lax.optimization_barrier((cot, normed))
    c_parts = [cot_b] + [zshift(cot_b, d) for d in (1, 2, 3)]
    normed_other = swap(normed)
    proj, agg, wall = project(normed, normed_other, weights)
    agg_all = lax.all_to_all(agg, "chan", 0, 0, axis_index_groups=SAME_CORE, tiled=True)

    gm_all = sum(
        dot_nt(c, lax.dynamic_slice_in_dim(out_weight, ((z + 4 - d) % 4) * 1024, 1024, 1))
        for d, c in enumerate(c_parts)
    )
    gm_mine = jnp.where(lead, gm_all[:, :256], gm_all[:, 256:])
    gm_other = jnp.where(lead, gm_all[:, 256:], gm_all[:, :256])
    gm = jnp.concatenate([gm_mine, swap(gm_other)], 0)

    mix_own, mix_oth, gg, gagg = across(proj, agg_all, gm)
    ragg = lax.all_to_all(gagg, "chan", 0, 0, axis_index_groups=SAME_CORE, tiled=True)

    mix_got = swap(mix_oth)
    mix = jnp.concatenate([jnp.where(lead, mix_own, mix_got), jnp.where(lead, mix_got, mix_own)], 1)
    part = dot_nn(mix, out_weight)

    def quarter(value, d):
        return lax.dynamic_slice_in_dim(value, ((z + d) % 4) * 1024, 1024, 1)

    part_b = part.astype(BF)
    summed = quarter(part, 0)
    for d in (1, 2, 3):
        summed = summed + zshift(quarter(part_b, d), d).astype(F32)
    layer_out = (summed + message[:128].astype(F32)).astype(BF)

    own2, oth2, stk, corr_own, corr_oth = backward(proj, gg, ragg, wall)
    got2 = swap(oth2)
    corr_got = swap(corr_oth)
    own_r, oth_r = rest(stk, wall)
    got_r = swap(oth_r)
    scal = (inv_rms, corr_own, corr_got)
    msg2, = call(one_kernel, [VM] * 6, [(VM, shape((128, 1024), BF))], (own2, got2, h_parts[2]) + scal)
    r2 = zshift(msg2, 2)
    msg1, msg3 = call(
        two_kernel, [VM] * 7, [(VM, shape((128, 1024), BF))] * 2,
        (own_r, got_r, h_parts[3], h_parts[1]) + scal,
    )
    r1 = zshift(msg1, 1)
    r3 = zshift(msg3, 3)
    input_grad, = call(
        last_kernel, [VM] * 10, [(VM, shape((128, 1024), BF))],
        (own_r, got_r, h_parts[0]) + scal + (cot, r1, r2, r3),
    )
    return layer_out.reshape(16, 8, 1024), input_grad.reshape(16, 8, 1024)


def solution(mesh):
    return jax.shard_map(
        layer,
        mesh=mesh,
        in_specs=(
            P("chan", "region", "head"),
            P("chan", "head"),
            P("head"),
            P(None, "chan", "head"),
            P("head", None),
            P("chan", "region", "head"),
        ),
        out_specs=(P("chan", "region", "head"), P("chan", "region", "head")),
        check_vma=False,
    )
```

```python
import jax
import jax.numpy as jnp
from jax import lax
from jax.experimental import pallas as pl
from jax.experimental.pallas import tpu as pltpu
from jax.sharding import PartitionSpec as P


F32 = jnp.float32
BF = jnp.bfloat16
NY, NX, NC, NZ = 4, 4, 2, 4
HD = 128
FAC = HD ** -0.5
CHG = 16
PAT = 8


def chan_id(y, x, c):
    return (y % NY) * (NX * NC) + (x % NX) * NC + (c % NC)


SITES = [(y, x, c) for y in range(NY) for x in range(NX) for c in range(NC)]
SWAP = [(chan_id(y, x, c), chan_id(y, x, c + 1)) for y, x, c in SITES]
SAME_CORE = [[chan_id(y, x, c) for y in range(NY) for x in range(NX)] for c in range(NC)]


def ring(first, step):
    pairs = []
    for y, x, c in SITES:
        if (c == 0) == first:
            pairs.append((chan_id(y, x, c), chan_id(y, x + step, c)))
        else:
            pairs.append((chan_id(y, x, c), chan_id(y + step, x, c)))
    return pairs


def swap(value):
    return lax.ppermute(value, "chan", SWAP)


def zshift(value, step):
    return lax.ppermute(value, "head", [(i, (i + step) % NZ) for i in range(NZ)])


def dot_nt(a, b):
    return lax.dot_general(a, b, (((1,), (1,)), ((), ())), preferred_element_type=F32)


def dot_nn(a, b):
    return lax.dot_general(a, b, (((1,), (0,)), ((), ())), preferred_element_type=F32)


def dot_tn(a, b):
    return lax.dot_general(a, b, (((0,), (0,)), ((), ())), preferred_element_type=F32)


def inv_norm(u):
    return lax.rsqrt(jnp.mean(u * u, axis=-1, keepdims=True) + 1e-06)


def norm_back(u, r, dy):
    return r * dy - u * (r * r * r * jnp.mean(dy * u, axis=-1, keepdims=True))


def same_patch(rows, cols):
    ri = lax.broadcasted_iota(jnp.int32, (rows, cols), 0) % PAT
    ci = lax.broadcasted_iota(jnp.int32, (rows, cols), 1) % PAT
    return ri == ci


def softmax_rows(scores, mask):
    e = jnp.where(mask, jnp.exp(scores), 0.0)
    return e / jnp.sum(e, axis=-1, keepdims=True)


def place():
    chan = lax.axis_index("chan")
    return chan // 8, (chan // 2) % 4, chan % 2, lax.axis_index("head")


def slot_of(off):
    return jnp.where(off == 3, 1, jnp.where(off == 1, 2, jnp.where(off == 2, 3, 0)))


def off_of(slot):
    return jnp.where(slot == 1, 3, jnp.where(slot == 2, 1, jnp.where(slot == 3, 2, 0)))


def within(proj, rows, h, mask):
    q = proj[rows, pl.ds(h * 128, 128)]
    k = proj[rows, pl.ds(256 + h * 128, 128)]
    v = proj[rows, pl.ds(512 + h * 128, 128)]
    qf = q.astype(F32)
    kf = k.astype(F32)
    rq = inv_norm(qf)
    rk = inv_norm(kf)
    kn = (kf * rk).astype(BF)
    w = softmax_rows(dot_nt(q, kn) * (rq * FAC), mask)
    return qf, kf, v, rq, rk, kn, w


def prepare_kernel(tokens, position, gain, message):
    hidden = tokens[...].astype(F32) + position[...].astype(F32)[:, None, :]
    message[0:128, :] = hidden.reshape(128, 1024).astype(BF)
    message[128:136, :] = jnp.broadcast_to(gain[...], (8, 1024))


def norm_kernel(p0, p1, p2, p3, normed, inv):
    parts = (p0, p1, p2, p3)
    square = jnp.zeros((128, 1), F32)
    for p in parts:
        h = p[0:128, :].astype(F32)
        square = square + jnp.sum(h * h, axis=-1, keepdims=True)
    r = lax.rsqrt(square * (1.0 / 4096) + 1e-05)
    inv[...] = jnp.broadcast_to(r, (128, 128))
    for n, p in enumerate(parts):
        for b in range(4):
            cols = pl.ds(b * 256, 256)
            h = p[0:128, cols].astype(F32)
            g = p[128:136, cols].astype(F32)[0:1]
            normed[n * 4 + b] = (h * r * g).astype(BF)


PIECES = (
    (0, 1), (1, 2), (3, 1), (4, 1), (8, 1), (5, 2), (9, 2), (7, 1), (11, 1),
    (12, "a"), (12, "b"), (13, 1), (14, 1), (15, "a"), (15, "b"),
)


def project_kernel(own, oth, *refs):
    pieces = refs[:15]
    proj, agg, wall, wv, acc, sems, out_sems = refs[15:]
    copies = []
    for n, (ref, (slot, size)) in enumerate(zip(pieces, PIECES)):
        if size == "a":
            dst = wv.at[slot, 0:1]
        elif size == "b":
            dst = wv.at[slot, 1:2]
        else:
            dst = wv.at[slot:slot + size]
        copy = pltpu.make_async_copy(ref, dst, sems.at[n])
        copy.start()
        copies.append(copy)
    y, x, core, z = place()
    lead = core == 0
    acc[...] = jnp.zeros_like(acc)

    def step(i, carry):
        s3 = off_of(i // 4)
        s1 = off_of(i % 4)
        by = (y + jnp.where(lead, s3, s1)) % 4
        bx = (x + jnp.where(lead, s1, s3)) % 4
        blk = ((z + 4 - by) % 4) * 4 + bx
        lhs = jnp.concatenate([own[blk], oth[blk]], 0)
        for j in range(3):
            w = wv[i, :, j].reshape(256, 256)
            acc[:, j * 256:(j + 1) * 256] += dot_nn(lhs, w)
        return carry

    for copy in copies[:9]:
        copy.wait()
    lax.fori_loop(0, 12, step, 0)
    for copy in copies[9:]:
        copy.wait()
    back = pltpu.make_async_copy(wv, wall, out_sems.at[0])
    back.start()
    lax.fori_loop(12, 16, step, 0)
    proj[...] = acc[...].astype(BF)
    mask = same_patch(128, 128)
    for g in range(2):
        for h in range(2):
            _, _, v, _, _, _, w = within(proj, pl.ds(g * 128, 128), h, mask)
            f = dot_nn(w.astype(BF), v)
            m = jnp.sum(f.reshape(CHG, PAT, HD), axis=0) * (1.0 / CHG)
            agg[:, h, pl.ds(g * PAT, PAT), :] = jnp.broadcast_to(m.astype(BF)[None], (16, PAT, HD))
    back.wait()


def across_kernel(proj, agg, gm, mix_own, mix_oth, gg, gagg):
    mask = same_patch(256, 256)
    small = same_patch(128, 128)
    for h in range(2):
        cols = pl.ds(h * 128, 128)
        q = proj[:, cols]
        qf = q.astype(F32)
        rq = inv_norm(qf)
        a = agg[:, h].reshape(256, HD)
        af = a.astype(F32)
        ra = inv_norm(af)
        an = (af * ra).astype(BF)
        s = dot_nt(q, an) * (rq * FAC)
        w = softmax_rows(s, mask)
        wb = w.astype(BF)
        second = dot_nn(wb, a)
        for g, ref in enumerate((mix_own, mix_oth)):
            fine = within(proj, pl.ds(g * 128, 128), h, small)
            first = dot_nn(fine[6].astype(BF), fine[2])
            ref[:, cols] = (first + second[g * 128:(g + 1) * 128]).astype(BF)
        gf = gm[:, cols]
        g = gf.astype(BF)
        dw = dot_nt(g, a)
        ds = w * (dw - jnp.sum(w * dw, axis=-1, keepdims=True)) * FAC
        dsb = ds.astype(BF)
        gg[:, cols] = gf
        gg[:, pl.ds(256 + h * 128, 128)] = norm_back(qf, rq, dot_nn(dsb, an))
        dan = dot_tn(dsb, (qf * rq).astype(BF))
        da = dot_tn(wb, g) + norm_back(af, ra, dan)
        gagg[:, h] = da.astype(BF).reshape(16, 16, HD)


def quarter_slots(d):
    y, x, core, z = place()
    by = (z + d) % 4
    py = slot_of((by + 4 - y) % 4)
    slots = []
    for bx in range(4):
        px = slot_of((bx + 4 - x) % 4)
        slots.append(jnp.where(core == 0, py * 4 + px, px * 4 + py))
    return slots


def fetch(wall, wv, sems, d, at):
    copies = []
    for bx, slot in enumerate(quarter_slots(d)):
        copy = pltpu.make_async_copy(wall.at[slot], wv.at[at + bx], sems.at[at + bx])
        copy.start()
        copies.append(copy)
    return copies


def block_product(stk, wv, n):
    r = jnp.zeros((256, 256), F32)
    for j in range(3):
        r = r + dot_nt(stk[:, j * 256:(j + 1) * 256], wv[n, :, j].reshape(256, 256))
    return r


def back_kernel(proj, gg, ragg, wall, own, oth, stk, corr_own, corr_oth, wv, sems):
    copies = fetch(wall, wv, sems, 2, 0)
    own_grad = jnp.sum(ragg[...].astype(F32), axis=0) * (1.0 / CHG)
    mask = same_patch(128, 128)
    for g, ref in enumerate((corr_own, corr_oth)):
        rows = pl.ds(g * 128, 128)
        total = jnp.zeros((128, 1), F32)
        for h in range(2):
            cols = pl.ds(h * 128, 128)
            qf, kf, v, rq, rk, kn, w = within(proj, rows, h, mask)
            og = own_grad[h, g * PAT:(g + 1) * PAT, :]
            gf = gg[rows, cols] + jnp.broadcast_to(og[None], (CHG, PAT, HD)).reshape(128, HD)
            gb = gf.astype(BF)
            dv = dot_tn(w.astype(BF), gb)
            dw = dot_nt(gb, v)
            ds = w * (dw - jnp.sum(w * dw, axis=-1, keepdims=True)) * FAC
            dsb = ds.astype(BF)
            dq = norm_back(qf, rq, dot_nn(dsb, kn)) + gg[rows, pl.ds(256 + h * 128, 128)]
            dk = norm_back(kf, rk, dot_tn(dsb, (qf * rq).astype(BF)))
            dq = dq.astype(BF)
            dk = dk.astype(BF)
            dv = dv.astype(BF)
            stk[rows, cols] = dq
            stk[rows, pl.ds(256 + h * 128, 128)] = dk
            stk[rows, pl.ds(512 + h * 128, 128)] = dv
            prod = dq.astype(F32) * qf + dk.astype(F32) * kf + dv.astype(F32) * v.astype(F32)
            total = total + jnp.sum(prod, axis=-1, keepdims=True)
        ref[...] = jnp.broadcast_to(total, (128, 128))
    for copy in copies:
        copy.wait()

    def step(bx, carry):
        r = block_product(stk, wv, bx)
        cols = pl.ds(pl.multiple_of(bx * 256, 256), 256)
        own[:, cols] = r[0:128].astype(BF)
        oth[:, cols] = r[128:256].astype(BF)
        return carry

    lax.fori_loop(0, 4, step, 0)


def rest_kernel(stk, wall, own, oth, wv, sems):
    copies = []
    for n, d in enumerate((1, 3, 0)):
        copies.append(fetch(wall, wv, sems, d, n * 4))
    for n in range(3):
        for copy in copies[n]:
            copy.wait()

        def step(bx, carry):
            r = block_product(stk, wv, n * 4 + bx)
            cols = pl.ds(pl.multiple_of(bx * 256, 256), 256)
            own[n, :, cols] = r[0:128].astype(BF)
            oth[n, :, cols] = r[128:256].astype(BF)
            return carry

        lax.fori_loop(0, 4, step, 0)


def combine(mine, got, part, inv, corr_own, corr_got):
    r = inv[:, 0:1]
    c = (corr_own[:, 0:1] + corr_got[:, 0:1]) * (r * (1.0 / 4096))
    h = part[0:128, :].astype(F32)
    g = part[128:136, :].astype(F32)[0:1]
    return r * (g * (mine.astype(F32) + got.astype(F32)) - h * c)


def one_kernel(mine, got, part, inv, corr_own, corr_got, out):
    out[...] = combine(mine[...], got[...], part, inv, corr_own, corr_got).astype(BF)


def two_kernel(mine, got, part_a, part_b, inv, corr_own, corr_got, out_a, out_b):
    out_a[...] = combine(mine[0], got[0], part_a, inv, corr_own, corr_got).astype(BF)
    out_b[...] = combine(mine[1], got[1], part_b, inv, corr_own, corr_got).astype(BF)


def last_kernel(mine, got, part, inv, corr_own, corr_got, cot, r1, r2, r3, out):
    grad = combine(mine[2], got[2], part, inv, corr_own, corr_got)
    grad = grad + r1[...].astype(F32) + r2[...].astype(F32) + r3[...].astype(F32)
    out[...] = (cot[...].astype(F32) + grad).astype(BF)


def gm_kernel(c0, c1, c2, c3, ow, mine, other):
    _, _, core, z = place()
    for ref, which in ((mine, core), (other, 1 - core)):
        rows = pl.ds(pl.multiple_of(which * 256, 256), 256)
        total = jnp.zeros((128, 256), F32)
        for d, c in enumerate((c0, c1, c2, c3)):
            cols = pl.ds(pl.multiple_of(((z + 4 - d) % 4) * 1024, 1024), 1024)
            total = total + dot_nt(c[...], ow[rows, cols])
        ref[...] = total


def out_quarter(mine, got, ow, d):
    _, _, core, z = place()
    cols = pl.ds(pl.multiple_of(((z + d) % 4) * 1024, 1024), 1024)
    rows = pl.ds(pl.multiple_of(core * 256, 256), 256)
    rows_got = pl.ds(pl.multiple_of((1 - core) * 256, 256), 256)
    return dot_nn(mine[...], ow[rows, cols]) + dot_nn(got[...], ow[rows_got, cols])


def out_first_kernel(mine, got, ow, o2):
    o2[...] = out_quarter(mine, got, ow, 2).astype(BF)


def out_rest_kernel(mine, got, ow, o1, o3, o0):
    o1[...] = out_quarter(mine, got, ow, 1).astype(BF)
    o3[...] = out_quarter(mine, got, ow, 3).astype(BF)
    o0[...] = out_quarter(mine, got, ow, 0)


VM = pl.BlockSpec(memory_space=pltpu.VMEM)
AN = pl.BlockSpec(memory_space=pl.ANY)
HB = pl.BlockSpec(memory_space=pltpu.HBM)
PARAMS = pltpu.CompilerParams(vmem_limit_bytes=16 * 1024 * 1024)


def shape(dims, dtype):
    return jax.ShapeDtypeStruct(dims, dtype)


def call(kernel, ins, outs, args, scratch=()):
    return pl.pallas_call(
        kernel,
        in_specs=ins,
        out_specs=[spec for spec, _ in outs],
        out_shape=[sh for _, sh in outs],
        scratch_shapes=list(scratch),
        compiler_params=PARAMS,
    )(*args)


BLOCK = (2, 3, 128, 256)


def prepare(tokens, position, gain):
    return call(prepare_kernel, [VM] * 3, [(VM, shape((136, 1024), BF))], (tokens, position, gain))[0]


def normalise(parts):
    return call(
        norm_kernel, [VM] * 4,
        [(VM, shape((16, 128, 256), BF)), (VM, shape((128, 128), F32))], parts,
    )


def project(own, oth, weights):
    return call(
        project_kernel, [VM, VM] + [AN] * 15,
        [(VM, shape((256, 768), BF)), (VM, shape((16, 2, 16, HD), BF)), (HB, pltpu.HBM((16,) + BLOCK, BF))],
        (own, oth) + weights,
        (
            pltpu.VMEM((16,) + BLOCK, BF), pltpu.VMEM((256, 768), F32),
            pltpu.SemaphoreType.DMA((15,)), pltpu.SemaphoreType.DMA((1,)),
        ),
    )


def across(proj, agg, gm):
    return call(
        across_kernel, [VM] * 3,
        [
            (VM, shape((128, 256), BF)), (VM, shape((128, 256), BF)),
            (VM, shape((256, 512), F32)), (VM, shape((16, 2, 16, HD), BF)),
        ],
        (proj, agg, gm),
    )


def backward(proj, gg, ragg, wall):
    return call(
        back_kernel, [VM] * 3 + [HB],
        [
            (VM, shape((128, 1024), BF)), (VM, shape((128, 1024), BF)), (VM, shape((256, 768), BF)),
            (VM, shape((128, 128), F32)), (VM, shape((128, 128), F32)),
        ],
        (proj, gg, ragg, pltpu.with_memory_space_constraint(wall, pltpu.HBM)),
        (pltpu.VMEM((4,) + BLOCK, BF), pltpu.SemaphoreType.DMA((4,))),
    )


def rest(stk, wall):
    return call(
        rest_kernel, [VM, HB],
        [(VM, shape((3, 128, 1024), BF)), (VM, shape((3, 128, 1024), BF))],
        (stk, pltpu.with_memory_space_constraint(wall, pltpu.HBM)),
        (pltpu.VMEM((12,) + BLOCK, BF), pltpu.SemaphoreType.DMA((12,))),
    )


def own_weights(qkv_weight, core):
    mine = lax.dynamic_slice_in_dim(qkv_weight, core * 256, 256, 2)
    other = lax.dynamic_slice_in_dim(qkv_weight, (1 - core) * 256, 256, 2)
    got = swap(other)
    lead = core == 0
    return jnp.stack([jnp.where(lead, mine, got), jnp.where(lead, got, mine)])


def gather_weights(own):
    def near(value, step):
        return lax.ppermute(value, "chan", ring(True, step))

    def cross(value, step):
        return lax.ppermute(value, "chan", ring(False, step))

    r = near(own, 1)
    l = near(own, -1)
    up = cross(own, 1)
    down = cross(own, -1)
    pair = jnp.stack([r, l])

    far = jnp.concatenate([near(r[:1], 1), near(l[1:], -1)], 0)
    pair_up = cross(pair, 1)
    pair_down = cross(pair, -1)
    over_a = cross(up[:1], 1)
    over_b = cross(down[1:], -1)
    far_up = cross(far, 1)
    far_down = cross(far, -1)
    pair_a = cross(pair_up[0], 1)
    pair_b = cross(pair_down[1], -1)
    far_a = cross(far_up[:1], 1)
    far_b = cross(far_down[1:], -1)

    def whole(value):
        return value.reshape((-1,) + value.shape[-4:])

    lead = tuple(whole(v) for v in (own, pair, far, up, down, pair_up, pair_down, far_up, far_down))
    tail = (over_a, over_b, whole(pair_a), whole(pair_b), far_a, far_b)
    return lead + tail, far


def layer(tokens, position, gain, qkv_weight, out_weight, cotangent):
    _, _, core, _ = place()

    own_w = own_weights(qkv_weight, core)
    message = prepare(tokens, position, gain.reshape(1, 1024))
    h_parts = [message]
    for d in (1, 2, 3):
        h_parts.append(zshift(message, d))
    weights, far = gather_weights(own_w)

    waited, _ = lax.optimization_barrier((h_parts, far))
    normed, inv_rms = normalise(waited)
    cot = cotangent.reshape(128, 1024)
    cot_b, normed = lax.optimization_barrier((cot, normed))
    c_parts = [cot_b]
    for d in (1, 2, 3):
        c_parts.append(zshift(cot_b, d))
    normed_other = swap(normed)
    proj, agg, wall = project(normed, normed_other, weights)
    agg_all = lax.all_to_all(agg, "chan", 0, 0, axis_index_groups=SAME_CORE, tiled=True)

    gm_mine, gm_other = call(
        gm_kernel, [VM] * 5, [(VM, shape((128, 256), F32))] * 2, c_parts + [out_weight],
    )
    gm = jnp.concatenate([gm_mine, swap(gm_other)], 0)

    mix_own, mix_oth, gg, gagg = across(proj, agg_all, gm)
    ragg = lax.all_to_all(gagg, "chan", 0, 0, axis_index_groups=SAME_CORE, tiled=True)

    mix_got = swap(mix_oth)
    o2, = call(
        out_first_kernel, [VM] * 3, [(VM, shape((128, 1024), BF))], (mix_own, mix_got, out_weight),
    )
    s2 = zshift(o2, 2)
    o1, o3, o0 = call(
        out_rest_kernel, [VM] * 3,
        [(VM, shape((128, 1024), BF)), (VM, shape((128, 1024), BF)), (VM, shape((128, 1024), F32))],
        (mix_own, mix_got, out_weight),
    )
    s1 = zshift(o1, 1)
    s3 = zshift(o3, 3)
    summed = o0 + s1.astype(F32) + s2.astype(F32) + s3.astype(F32)
    layer_out = (summed + message[:128].astype(F32)).astype(BF)

    own2, oth2, stk, corr_own, corr_oth = backward(proj, gg, ragg, wall)
    got2 = swap(oth2)
    corr_got = swap(corr_oth)
    own_r, oth_r = rest(stk, wall)
    got_r = swap(oth_r)
    scal = (inv_rms, corr_own, corr_got)
    msg2, = call(one_kernel, [VM] * 6, [(VM, shape((128, 1024), BF))], (own2, got2, h_parts[2]) + scal)
    r2 = zshift(msg2, 2)
    msg1, msg3 = call(
        two_kernel, [VM] * 7, [(VM, shape((128, 1024), BF))] * 2,
        (own_r, got_r, h_parts[3], h_parts[1]) + scal,
    )
    r1 = zshift(msg1, 1)
    r3 = zshift(msg3, 3)
    input_grad, = call(
        last_kernel, [VM] * 10, [(VM, shape((128, 1024), BF))],
        (own_r, got_r, h_parts[0]) + scal + (cot, r1, r2, r3),
    )
    return layer_out.reshape(16, 8, 1024), input_grad.reshape(16, 8, 1024)


def solution(mesh):
    return jax.shard_map(
        layer,
        mesh=mesh,
        in_specs=(
            P("chan", "region", "head"),
            P("chan", "head"),
            P("head"),
            P(None, "chan", "head"),
            P("head", None),
            P("chan", "region", "head"),
        ),
        out_specs=(P("chan", "region", "head"), P("chan", "region", "head")),
        check_vma=False,
    )
```

```python
import jax
import jax.numpy as jnp
from jax import lax
from jax.experimental import pallas as pl
from jax.experimental.pallas import tpu as pltpu
from jax.sharding import PartitionSpec as P


F32 = jnp.float32
BF = jnp.bfloat16
NY, NX, NC, NZ = 4, 4, 2, 4
HD = 128
FAC = HD ** -0.5
CHG = 16
PAT = 8


def chan_id(y, x, c):
    return (y % NY) * (NX * NC) + (x % NX) * NC + (c % NC)


SITES = [(y, x, c) for y in range(NY) for x in range(NX) for c in range(NC)]
SWAP = [(chan_id(y, x, c), chan_id(y, x, c + 1)) for y, x, c in SITES]
SAME_CORE = [[chan_id(y, x, c) for y in range(NY) for x in range(NX)] for c in range(NC)]


def ring(first, step):
    pairs = []
    for y, x, c in SITES:
        if (c == 0) == first:
            pairs.append((chan_id(y, x, c), chan_id(y, x + step, c)))
        else:
            pairs.append((chan_id(y, x, c), chan_id(y + step, x, c)))
    return pairs


def swap(value):
    return lax.ppermute(value, "chan", SWAP)


def zshift(value, step):
    return lax.ppermute(value, "head", [(i, (i + step) % NZ) for i in range(NZ)])


def dot_nt(a, b):
    return lax.dot_general(a, b, (((1,), (1,)), ((), ())), preferred_element_type=F32)


def dot_nn(a, b):
    return lax.dot_general(a, b, (((1,), (0,)), ((), ())), preferred_element_type=F32)


def dot_tn(a, b):
    return lax.dot_general(a, b, (((0,), (0,)), ((), ())), preferred_element_type=F32)


def inv_norm(u):
    return lax.rsqrt(jnp.mean(u * u, axis=-1, keepdims=True) + 1e-06)


def norm_back(u, r, dy):
    return r * dy - u * (r * r * r * jnp.mean(dy * u, axis=-1, keepdims=True))


def same_patch(rows, cols):
    ri = lax.broadcasted_iota(jnp.int32, (rows, cols), 0) % PAT
    ci = lax.broadcasted_iota(jnp.int32, (rows, cols), 1) % PAT
    return ri == ci


def softmax_rows(scores, mask):
    e = jnp.where(mask, jnp.exp(scores), 0.0)
    return e / jnp.sum(e, axis=-1, keepdims=True)


def place():
    chan = lax.axis_index("chan")
    return chan // 8, (chan // 2) % 4, chan % 2, lax.axis_index("head")


def slot_of(off):
    return jnp.where(off == 3, 1, jnp.where(off == 1, 2, jnp.where(off == 2, 3, 0)))


def within(proj, rows, h, mask):
    q = proj[rows, pl.ds(h * 128, 128)]
    k = proj[rows, pl.ds(256 + h * 128, 128)]
    v = proj[rows, pl.ds(512 + h * 128, 128)]
    qf = q.astype(F32)
    kf = k.astype(F32)
    rq = inv_norm(qf)
    rk = inv_norm(kf)
    kn = (kf * rk).astype(BF)
    w = softmax_rows(dot_nt(q, kn) * (rq * FAC), mask)
    return qf, kf, v, rq, rk, kn, w


def prepare_kernel(tokens, position, gain, message, tok, pos, gn, sems):
    copies = [
        pltpu.make_async_copy(tokens, tok, sems.at[0]),
        pltpu.make_async_copy(position, pos, sems.at[1]),
        pltpu.make_async_copy(gain, gn, sems.at[2]),
    ]
    for copy in copies:
        copy.start()
    for copy in copies:
        copy.wait()
    hidden = tok[...].astype(F32) + pos[...].astype(F32)[:, None, :]
    message[0:128, :] = hidden.reshape(128, 1024).astype(BF)
    message[128:136, :] = jnp.broadcast_to(gn[...][None], (8, 1024))


def norm_kernel(p0, p1, p2, p3, normed, inv):
    parts = (p0, p1, p2, p3)
    square = jnp.zeros((128, 1), F32)
    for p in parts:
        h = p[0:128, :].astype(F32)
        square = square + jnp.sum(h * h, axis=-1, keepdims=True)
    r = lax.rsqrt(square * (1.0 / 4096) + 1e-05)
    inv[...] = jnp.broadcast_to(r, (128, 128))
    for n, p in enumerate(parts):
        for b in range(4):
            cols = pl.ds(b * 256, 256)
            h = p[0:128, cols].astype(F32)
            g = p[128:136, cols].astype(F32)[0:1]
            normed[n * 4 + b] = (h * r * g).astype(BF)


EARLY = ((0, 1), (1, 2), (3, 1), (4, 1), (8, 1), (5, 2), (9, 2), (7, 1), (11, 1))
LATE = ((0, "a"), (0, "b"), (1, 1), (2, 1), (3, "a"), (3, "b"))


def load_pieces(pieces, places, wv, sems):
    copies = []
    for n, (ref, (slot, size)) in enumerate(zip(pieces, places)):
        if size == "a":
            dst = wv.at[slot, 0:1]
        elif size == "b":
            dst = wv.at[slot, 1:2]
        else:
            dst = wv.at[slot:slot + size]
        copy = pltpu.make_async_copy(ref, dst, sems.at[n])
        copy.start()
        copies.append(copy)
    return copies


def group_lhs(own, oth, s3):
    y, x, core, z = place()
    lead = core == 0
    parts = []
    for s1 in (0, 3, 1, 2):
        by = (y + jnp.where(lead, s3, s1)) % 4
        bx = (x + jnp.where(lead, s1, s3)) % 4
        blk = ((z + 4 - by) % 4) * 4 + bx
        parts.append(jnp.concatenate([own[blk], oth[blk]], 0))
    return jnp.concatenate(parts, 1)


def project_early_kernel(own, oth, *refs):
    pieces = refs[:9]
    acc, wall, wv, sems, out_sem = refs[9:]
    copies = load_pieces(pieces, EARLY, wv, sems)
    for n, group in enumerate(((0, 1, 2), (3, 5, 7), (4, 6, 8))):
        for at in group:
            copies[at].wait()
        lhs = group_lhs(own, oth, (0, 3, 1)[n])
        for j in range(3):
            cols = slice(j * 256, (j + 1) * 256)
            r = dot_nn(lhs, wv[n * 4:n * 4 + 4, :, j].reshape(1024, 256))
            if n == 0:
                acc[:, cols] = r
            else:
                acc[:, cols] += r
    back = pltpu.make_async_copy(wv, wall.at[0:12], out_sem.at[0])
    back.start()
    back.wait()


def project_late_kernel(own, oth, acc, wall_in, *refs):
    pieces = refs[:6]
    proj, agg, wall, wv, sems, out_sem = refs[6:]
    copies = load_pieces(pieces, LATE, wv, sems)
    lhs = group_lhs(own, oth, 2)
    for copy in copies:
        copy.wait()
    back = pltpu.make_async_copy(wv, wall.at[12:16], out_sem.at[0])
    back.start()
    for j in range(3):
        cols = slice(j * 256, (j + 1) * 256)
        r = dot_nn(lhs, wv[:, :, j].reshape(1024, 256))
        proj[:, cols] = (acc[:, cols] + r).astype(BF)
    mask = same_patch(128, 128)
    for g in range(2):
        for h in range(2):
            _, _, v, _, _, _, w = within(proj, pl.ds(g * 128, 128), h, mask)
            f = dot_nn(w.astype(BF), v)
            m = jnp.sum(f.reshape(CHG, PAT, HD), axis=0) * (1.0 / CHG)
            agg[:, h, pl.ds(g * PAT, PAT), :] = jnp.broadcast_to(m.astype(BF)[None], (16, PAT, HD))
    back.wait()


def across_kernel(proj, agg, mix_own, mix_oth, soft):
    mask = same_patch(256, 256)
    small = same_patch(128, 128)
    for h in range(2):
        cols = pl.ds(h * 128, 128)
        q = proj[:, cols]
        rq = inv_norm(q.astype(F32))
        a = agg[:, h].reshape(256, HD)
        af = a.astype(F32)
        an = (af * inv_norm(af)).astype(BF)
        w = softmax_rows(dot_nt(q, an) * (rq * FAC), mask)
        soft[h] = w
        second = dot_nn(w.astype(BF), a)
        for g, ref in enumerate((mix_own, mix_oth)):
            fine = within(proj, pl.ds(g * 128, 128), h, small)
            first = dot_nn(fine[6].astype(BF), fine[2])
            ref[:, cols] = (first + second[g * 128:(g + 1) * 128]).astype(BF)


def across_back_kernel(proj, agg, gm_mine, gm_got, soft, ow, gg, gagg, ow_near, sem):
    copy = pltpu.make_async_copy(ow, ow_near, sem.at[0])
    copy.start()
    for h in range(2):
        cols = pl.ds(h * 128, 128)
        qf = proj[:, cols].astype(F32)
        rq = inv_norm(qf)
        a = agg[:, h].reshape(256, HD)
        af = a.astype(F32)
        ra = inv_norm(af)
        an = (af * ra).astype(BF)
        w = soft[h]
        wb = w.astype(BF)
        gf = jnp.concatenate([gm_mine[:, cols], gm_got[:, cols]], 0)
        g = gf.astype(BF)
        dw = dot_nt(g, a)
        ds = w * (dw - jnp.sum(w * dw, axis=-1, keepdims=True)) * FAC
        dsb = ds.astype(BF)
        gg[:, cols] = gf
        gg[:, pl.ds(256 + h * 128, 128)] = norm_back(qf, rq, dot_nn(dsb, an))
        dan = dot_tn(dsb, (qf * rq).astype(BF))
        da = dot_tn(wb, g) + norm_back(af, ra, dan)
        gagg[:, h] = da.astype(BF).reshape(16, 16, HD)
    copy.wait()


def quarter_slots(d):
    y, x, core, z = place()
    by = (z + d) % 4
    py = slot_of((by + 4 - y) % 4)
    slots = []
    for bx in range(4):
        px = slot_of((bx + 4 - x) % 4)
        slots.append(jnp.where(core == 0, py * 4 + px, px * 4 + py))
    return slots


def fetch(wall, wv, sems, d, at):
    copies = []
    for bx, slot in enumerate(quarter_slots(d)):
        copy = pltpu.make_async_copy(wall.at[slot], wv.at[at + bx], sems.at[at + bx])
        copy.start()
        copies.append(copy)
    return copies


def block_product(stk, wv, n):
    w = jnp.concatenate([wv[n, :, j].reshape(256, 256) for j in range(3)], 1)
    return dot_nt(stk[...], w)


def back_kernel(proj, gg, ragg, wall, own, oth, stk, corr_own, corr_oth, wv, sems):
    copies = fetch(wall, wv, sems, 2, 0)
    own_grad = jnp.sum(ragg[...].astype(F32), axis=0) * (1.0 / CHG)
    mask = same_patch(128, 128)
    for g, ref in enumerate((corr_own, corr_oth)):
        rows = pl.ds(g * 128, 128)
        total = jnp.zeros((128, 1), F32)
        for h in range(2):
            cols = pl.ds(h * 128, 128)
            qf, kf, v, rq, rk, kn, w = within(proj, rows, h, mask)
            og = own_grad[h, g * PAT:(g + 1) * PAT, :]
            gf = gg[rows, cols] + jnp.broadcast_to(og[None], (CHG, PAT, HD)).reshape(128, HD)
            gb = gf.astype(BF)
            dv = dot_tn(w.astype(BF), gb)
            dw = dot_nt(gb, v)
            ds = w * (dw - jnp.sum(w * dw, axis=-1, keepdims=True)) * FAC
            dsb = ds.astype(BF)
            dq = norm_back(qf, rq, dot_nn(dsb, kn)) + gg[rows, pl.ds(256 + h * 128, 128)]
            dk = norm_back(kf, rk, dot_tn(dsb, (qf * rq).astype(BF)))
            dq = dq.astype(BF)
            dk = dk.astype(BF)
            dv = dv.astype(BF)
            stk[rows, cols] = dq
            stk[rows, pl.ds(256 + h * 128, 128)] = dk
            stk[rows, pl.ds(512 + h * 128, 128)] = dv
            prod = dq.astype(F32) * qf + dk.astype(F32) * kf + dv.astype(F32) * v.astype(F32)
            total = total + jnp.sum(prod, axis=-1, keepdims=True)
        ref[...] = jnp.broadcast_to(total, (128, 128))
    for copy in copies:
        copy.wait()

    def step(bx, carry):
        r = block_product(stk, wv, bx)
        cols = pl.ds(pl.multiple_of(bx * 256, 256), 256)
        own[:, cols] = r[0:128].astype(BF)
        oth[:, cols] = r[128:256].astype(BF)
        return carry

    lax.fori_loop(0, 4, step, 0)


def rest_kernel(stk, wall, own, oth, wv, sems):
    copies = []
    for n, d in enumerate((1, 3, 0)):
        copies.append(fetch(wall, wv, sems, d, n * 4))
    for n in range(3):
        for copy in copies[n]:
            copy.wait()

        def step(bx, carry):
            r = block_product(stk, wv, n * 4 + bx)
            cols = pl.ds(pl.multiple_of(bx * 256, 256), 256)
            own[n, :, cols] = r[0:128].astype(BF)
            oth[n, :, cols] = r[128:256].astype(BF)
            return carry

        lax.fori_loop(0, 4, step, 0)


def combine(mine, got, part, inv, corr_own, corr_got):
    r = inv[:, 0:1]
    c = (corr_own[:, 0:1] + corr_got[:, 0:1]) * (r * (1.0 / 4096))
    h = part[0:128, :].astype(F32)
    g = part[128:136, :].astype(F32)[0:1]
    return r * (g * (mine.astype(F32) + got.astype(F32)) - h * c)


def one_kernel(mine, got, part, inv, corr_own, corr_got, out):
    out[...] = combine(mine[...], got[...], part, inv, corr_own, corr_got).astype(BF)


def two_kernel(mine, got, part_a, part_b, inv, corr_own, corr_got, out_a, out_b):
    out_a[...] = combine(mine[0], got[0], part_a, inv, corr_own, corr_got).astype(BF)
    out_b[...] = combine(mine[1], got[1], part_b, inv, corr_own, corr_got).astype(BF)


def last_kernel(mine, got, part, inv, corr_own, corr_got, cot, r1, r2, r3, out):
    grad = combine(mine[2], got[2], part, inv, corr_own, corr_got)
    grad = grad + r1[...].astype(F32) + r2[...].astype(F32) + r3[...].astype(F32)
    out[...] = (cot[...].astype(F32) + grad).astype(BF)


def gm_kernel(c0, c1, c2, c3, ow, mine, other):
    _, _, core, z = place()
    for ref, which in ((mine, core), (other, 1 - core)):
        rows = pl.ds(pl.multiple_of(which * 256, 256), 256)
        total = jnp.zeros((128, 256), F32)
        for d, c in enumerate((c0, c1, c2, c3)):
            cols = pl.ds(pl.multiple_of(((z + 4 - d) % 4) * 1024, 1024), 1024)
            total = total + dot_nt(c[...], ow[rows, cols])
        ref[...] = total


def out_quarter(mine, got, ow, d):
    _, _, core, z = place()
    cols = pl.ds(pl.multiple_of(((z + d) % 4) * 1024, 1024), 1024)
    rows = pl.ds(pl.multiple_of(core * 256, 256), 256)
    rows_got = pl.ds(pl.multiple_of((1 - core) * 256, 256), 256)
    return dot_nn(mine[...], ow[rows, cols]) + dot_nn(got[...], ow[rows_got, cols])


def out_first_kernel(mine, got, ow, o2):
    o2[...] = out_quarter(mine, got, ow, 2).astype(BF)


def out_rest_kernel(mine, got, ow, o1, o3, o0):
    o1[...] = out_quarter(mine, got, ow, 1).astype(BF)
    o3[...] = out_quarter(mine, got, ow, 3).astype(BF)
    o0[...] = out_quarter(mine, got, ow, 0)


VM = pl.BlockSpec(memory_space=pltpu.VMEM)
AN = pl.BlockSpec(memory_space=pl.ANY)
HB = pl.BlockSpec(memory_space=pltpu.HBM)
PARAMS = pltpu.CompilerParams(vmem_limit_bytes=16 * 1024 * 1024)


def shape(dims, dtype):
    return jax.ShapeDtypeStruct(dims, dtype)


def call(kernel, ins, outs, args, scratch=()):
    return pl.pallas_call(
        kernel,
        in_specs=ins,
        out_specs=[spec for spec, _ in outs],
        out_shape=[sh for _, sh in outs],
        scratch_shapes=list(scratch),
        compiler_params=PARAMS,
    )(*args)


BLOCK = (2, 3, 128, 256)


def in_hbm(value):
    return pltpu.with_memory_space_constraint(value, pltpu.HBM)


def prepare(tokens, position, gain):
    return call(
        prepare_kernel, [HB] * 3, [(VM, shape((136, 1024), BF))],
        (in_hbm(tokens), in_hbm(position), in_hbm(gain)),
        (
            pltpu.VMEM((16, 8, 1024), BF), pltpu.VMEM((16, 1024), BF), pltpu.VMEM((1024,), BF),
            pltpu.SemaphoreType.DMA((3,)),
        ),
    )[0]


def normalise(parts):
    return call(
        norm_kernel, [VM] * 4,
        [(VM, shape((16, 128, 256), BF)), (VM, shape((128, 128), F32))], parts,
    )


WALL = pltpu.HBM((16,) + BLOCK, BF)


def project_early(own, oth, weights):
    return call(
        project_early_kernel, [VM, VM] + [AN] * 9,
        [(VM, shape((256, 768), F32)), (HB, WALL)],
        (own, oth) + weights,
        (pltpu.VMEM((12,) + BLOCK, BF), pltpu.SemaphoreType.DMA((9,)), pltpu.SemaphoreType.DMA((1,))),
    )


def project_late(own, oth, acc, wall, weights):
    return pl.pallas_call(
        project_late_kernel,
        in_specs=[VM, VM, VM, HB] + [AN] * 6,
        out_specs=[VM, VM, HB],
        out_shape=[shape((256, 768), BF), shape((16, 2, 16, HD), BF), WALL],
        scratch_shapes=[pltpu.VMEM((4,) + BLOCK, BF), pltpu.SemaphoreType.DMA((6,)), pltpu.SemaphoreType.DMA((1,))],
        input_output_aliases={3: 2},
        compiler_params=PARAMS,
        name="late",
    )(own, oth, acc, in_hbm(wall), *weights)


def across(proj, agg):
    return call(
        across_kernel, [VM] * 2,
        [(VM, shape((128, 256), BF)), (VM, shape((128, 256), BF)), (VM, shape((2, 256, 256), F32))],
        (proj, agg),
    )


def across_back(proj, agg, gm_mine, gm_got, soft, out_weight):
    return call(
        across_back_kernel, [VM] * 5 + [HB],
        [(VM, shape((256, 512), F32)), (VM, shape((16, 2, 16, HD), BF)), (VM, shape((512, 4096), BF))],
        (proj, agg, gm_mine, gm_got, soft, in_hbm(out_weight)),
        (pltpu.SemaphoreType.DMA((1,)),),
    )


def backward(proj, gg, ragg, wall):
    return call(
        back_kernel, [VM] * 3 + [HB],
        [
            (VM, shape((128, 1024), BF)), (VM, shape((128, 1024), BF)), (VM, shape((256, 768), BF)),
            (VM, shape((128, 128), F32)), (VM, shape((128, 128), F32)),
        ],
        (proj, gg, ragg, in_hbm(wall)),
        (pltpu.VMEM((4,) + BLOCK, BF), pltpu.SemaphoreType.DMA((4,))),
    )


def rest(stk, wall):
    return call(
        rest_kernel, [VM, HB],
        [(VM, shape((3, 128, 1024), BF)), (VM, shape((3, 128, 1024), BF))],
        (stk, in_hbm(wall)),
        (pltpu.VMEM((12,) + BLOCK, BF), pltpu.SemaphoreType.DMA((12,))),
    )


def own_weights(qkv_weight, core):
    mine = lax.dynamic_slice_in_dim(qkv_weight, core * 256, 256, 2)
    other = lax.dynamic_slice_in_dim(qkv_weight, (1 - core) * 256, 256, 2)
    got = swap(other)
    lead = core == 0
    return jnp.stack([jnp.where(lead, mine, got), jnp.where(lead, got, mine)])


def gather_weights(own):
    def near(value, step):
        return lax.ppermute(value, "chan", ring(True, step))

    def cross(value, step):
        return lax.ppermute(value, "chan", ring(False, step))

    r = near(own, 1)
    l = near(own, -1)

    up = cross(own, 1)
    down = cross(own, -1)
    pair = jnp.stack([r, l])
    far = jnp.concatenate([near(r[:1], 1), near(l[1:], -1)], 0)
    pair_up = cross(pair, 1)
    pair_down = cross(pair, -1)
    over_a = cross(up[:1], 1)
    over_b = cross(down[1:], -1)
    far_up = cross(far, 1)
    far_down = cross(far, -1)
    pair_a = cross(pair_up[0], 1)
    pair_b = cross(pair_down[1], -1)
    far_a = cross(far_up[:1], 1)
    far_b = cross(far_down[1:], -1)

    def whole(value):
        return value.reshape((-1,) + value.shape[-4:])

    lead = tuple(whole(v) for v in (own, pair, far, up, down, pair_up, pair_down, far_up, far_down))
    tail = (over_a, over_b, whole(pair_a), whole(pair_b), far_a, far_b)
    return lead, tail, far


def layer(tokens, position, gain, qkv_weight, out_weight, cotangent):
    _, _, core, _ = place()

    own_w = own_weights(qkv_weight, core)
    message = prepare(tokens, position, gain)
    h_parts = [message]
    for d in (1, 2, 3):
        h_parts.append(zshift(message, d))
    early, late, far = gather_weights(own_w)

    waited, _ = lax.optimization_barrier((h_parts, far))
    normed, inv_rms = normalise(waited)
    cot = cotangent.reshape(128, 1024)
    cot_b, normed = lax.optimization_barrier((cot, normed))
    c_parts = [cot_b]
    for d in (1, 2, 3):
        c_parts.append(zshift(cot_b, d))
    normed_other = swap(normed)
    acc, wall = project_early(normed, normed_other, early)
    proj, agg, wall = project_late(normed, normed_other, acc, wall, late)
    agg_all = lax.all_to_all(agg, "chan", 0, 0, axis_index_groups=SAME_CORE, tiled=True)

    gm_mine, gm_other = call(
        gm_kernel, [VM] * 5, [(VM, shape((128, 256), F32))] * 2, c_parts + [out_weight],
    )
    gm_got = swap(gm_other)

    mix_own, mix_oth, soft = across(proj, agg_all)
    mix_got = swap(mix_oth)
    gg, gagg, ow_near = across_back(proj, agg_all, gm_mine, gm_got, soft, out_weight)
    ragg = lax.all_to_all(gagg, "chan", 0, 0, axis_index_groups=SAME_CORE, tiled=True)

    o2, = call(
        out_first_kernel, [VM] * 3, [(VM, shape((128, 1024), BF))], (mix_own, mix_got, ow_near),
    )
    s2 = zshift(o2, 2)
    o1, o3, o0 = call(
        out_rest_kernel, [VM] * 3,
        [(VM, shape((128, 1024), BF)), (VM, shape((128, 1024), BF)), (VM, shape((128, 1024), F32))],
        (mix_own, mix_got, ow_near),
    )
    s1 = zshift(o1, 1)
    s3 = zshift(o3, 3)
    summed = o0 + s1.astype(F32) + s2.astype(F32) + s3.astype(F32)
    layer_out = (summed + message[:128].astype(F32)).astype(BF)

    own2, oth2, stk, corr_own, corr_oth = backward(proj, gg, ragg, wall)
    got2 = swap(oth2)
    corr_got = swap(corr_oth)
    own_r, oth_r = rest(stk, wall)
    got_r = swap(oth_r)
    scal = (inv_rms, corr_own, corr_got)
    msg2, = call(one_kernel, [VM] * 6, [(VM, shape((128, 1024), BF))], (own2, got2, h_parts[2]) + scal)
    r2 = zshift(msg2, 2)
    msg1, msg3 = call(
        two_kernel, [VM] * 7, [(VM, shape((128, 1024), BF))] * 2,
        (own_r, got_r, h_parts[3], h_parts[1]) + scal,
    )
    r1 = zshift(msg1, 1)
    r3 = zshift(msg3, 3)
    input_grad, = call(
        last_kernel, [VM] * 10, [(VM, shape((128, 1024), BF))],
        (own_r, got_r, h_parts[0]) + scal + (cot, r1, r2, r3),
    )
    return layer_out.reshape(16, 8, 1024), input_grad.reshape(16, 8, 1024)


def solution(mesh):
    return jax.shard_map(
        layer,
        mesh=mesh,
        in_specs=(
            P("chan", "region", "head"),
            P("chan", "head"),
            P("head"),
            P(None, "chan", "head"),
            P("head", None),
            P("chan", "region", "head"),
        ),
        out_specs=(P("chan", "region", "head"), P("chan", "region", "head")),
        check_vma=False,
    )
```

```python
import jax
import jax.numpy as jnp
from jax import lax
from jax.experimental import pallas as pl
from jax.experimental.pallas import tpu as pltpu
from jax.sharding import PartitionSpec as P


F32 = jnp.float32
BF = jnp.bfloat16
NY, NX, NC, NZ = 4, 4, 2, 4
HD = 128
FAC = HD ** -0.5
CHG = 16
PAT = 8


def chan_id(y, x, c):
    return (y % NY) * (NX * NC) + (x % NX) * NC + (c % NC)


SITES = [(y, x, c) for y in range(NY) for x in range(NX) for c in range(NC)]
SWAP = [(chan_id(y, x, c), chan_id(y, x, c + 1)) for y, x, c in SITES]
SAME_CORE = [[chan_id(y, x, c) for y in range(NY) for x in range(NX)] for c in range(NC)]


def ring(first, step):
    pairs = []
    for y, x, c in SITES:
        if (c == 0) == first:
            pairs.append((chan_id(y, x, c), chan_id(y, x + step, c)))
        else:
            pairs.append((chan_id(y, x, c), chan_id(y + step, x, c)))
    return pairs


def swap(value):
    return lax.ppermute(value, "chan", SWAP)


def zshift(value, step):
    return lax.ppermute(value, "head", [(i, (i + step) % NZ) for i in range(NZ)])


def dot_nt(a, b):
    return lax.dot_general(a, b, (((1,), (1,)), ((), ())), preferred_element_type=F32)


def dot_nn(a, b):
    return lax.dot_general(a, b, (((1,), (0,)), ((), ())), preferred_element_type=F32)


def dot_tn(a, b):
    return lax.dot_general(a, b, (((0,), (0,)), ((), ())), preferred_element_type=F32)


def inv_norm(u):
    return lax.rsqrt(jnp.mean(u * u, axis=-1, keepdims=True) + 1e-06)


def norm_back(u, r, dy):
    return r * dy - u * (r * r * r * jnp.mean(dy * u, axis=-1, keepdims=True))


def same_patch(rows, cols):
    ri = lax.broadcasted_iota(jnp.int32, (rows, cols), 0) % PAT
    ci = lax.broadcasted_iota(jnp.int32, (rows, cols), 1) % PAT
    return ri == ci


def softmax_rows(scores, mask):
    e = jnp.where(mask, jnp.exp(scores), 0.0)
    return e * (1.0 / jnp.sum(e, axis=-1, keepdims=True))


def place():
    chan = lax.axis_index("chan")
    return chan // 8, (chan // 2) % 4, chan % 2, lax.axis_index("head")


def slot_of(off):
    return jnp.where(off == 3, 1, jnp.where(off == 1, 2, jnp.where(off == 2, 3, 0)))


def within(proj, rows, h, mask):
    q = proj[rows, pl.ds(h * 128, 128)]
    k = proj[rows, pl.ds(256 + h * 128, 128)]
    v = proj[rows, pl.ds(512 + h * 128, 128)]
    qf = q.astype(F32)
    kf = k.astype(F32)
    rq = inv_norm(qf)
    rk = inv_norm(kf)
    kn = (kf * rk).astype(BF)
    w = softmax_rows(dot_nt(q, kn) * (rq * FAC), mask)
    return qf, kf, v, rq, rk, kn, w


def prepare_kernel(tokens, position, gain, message, tok, pos, gn, sems):
    copies = [
        pltpu.make_async_copy(tokens, tok, sems.at[0]),
        pltpu.make_async_copy(position, pos, sems.at[1]),
        pltpu.make_async_copy(gain, gn, sems.at[2]),
    ]
    for copy in copies:
        copy.start()
    for copy in copies:
        copy.wait()
    hidden = tok[...].astype(F32) + pos[...].astype(F32)[:, None, :]
    message[0:128, :] = hidden.reshape(128, 1024).astype(BF)
    message[128:136, :] = jnp.broadcast_to(gn[...][None], (8, 1024))


def norm_kernel(p0, p1, p2, p3, normed, inv):
    parts = (p0, p1, p2, p3)
    square = jnp.zeros((128, 1), F32)
    for p in parts:
        h = p[0:128, :].astype(F32)
        square = square + jnp.sum(h * h, axis=-1, keepdims=True)
    r = lax.rsqrt(square * (1.0 / 4096) + 1e-05)
    inv[...] = jnp.broadcast_to(r, (128, 128))
    for n, p in enumerate(parts):
        for b in range(4):
            cols = pl.ds(b * 256, 256)
            h = p[0:128, cols].astype(F32)
            g = p[128:136, cols].astype(F32)[0:1]
            normed[n * 4 + b] = (h * r * g).astype(BF)


EARLY = ((0, 1), (1, 2), (3, 1), (4, 1), (8, 1), (5, 2), (9, 2), (7, 1), (11, 1))
LATE = ((0, "a"), (0, "b"), (1, 1), (2, 1), (3, "a"), (3, "b"))


def save_pieces(pieces, places, wall, base, sems):
    copies = []
    for n, (ref, (slot, size)) in enumerate(zip(pieces, places)):
        if size == "a":
            dst = wall.at[base + slot, 0:1]
        elif size == "b":
            dst = wall.at[base + slot, 1:2]
        else:
            dst = wall.at[base + slot:base + slot + size]
        copy = pltpu.make_async_copy(ref, dst, sems.at[n])
        copy.start()
        copies.append(copy)
    return copies


def rows_of(pieces, j):
    parts = []
    for ref in pieces:
        if len(ref.shape) == 4:
            parts.append(ref[0, j])
        else:
            parts.append(ref[:, :, j].reshape(-1, 256))
    return jnp.concatenate(parts, 0)


def group_lhs(own, oth, s3):
    y, x, core, z = place()
    lead = core == 0
    parts = []
    for s1 in (0, 3, 1, 2):
        by = (y + jnp.where(lead, s3, s1)) % 4
        bx = (x + jnp.where(lead, s1, s3)) % 4
        blk = ((z + 4 - by) % 4) * 4 + bx
        parts.append(jnp.concatenate([own[blk], oth[blk]], 0))
    return jnp.concatenate(parts, 1)


def project_early_kernel(own, oth, *refs):
    pieces = refs[:9]
    acc, wall, sems = refs[9:]
    copies = save_pieces(pieces, EARLY, wall, 0, sems)
    for n, group in enumerate(((0, 1, 2), (3, 5, 7), (4, 6, 8))):
        lhs = group_lhs(own, oth, (0, 3, 1)[n])
        for j in range(3):
            cols = slice(j * 256, (j + 1) * 256)
            r = dot_nn(lhs, rows_of([pieces[at] for at in group], j))
            if n == 0:
                acc[:, cols] = r
            else:
                acc[:, cols] += r
    for copy in copies:
        copy.wait()


def project_late_kernel(own, oth, acc, wall_in, *refs):
    pieces = refs[:6]
    proj, agg, wall, sems = refs[6:]
    copies = save_pieces(pieces, LATE, wall, 12, sems)
    lhs = group_lhs(own, oth, 2)
    for j in range(3):
        cols = slice(j * 256, (j + 1) * 256)
        r = dot_nn(lhs, rows_of(pieces, j))
        proj[:, cols] = (acc[:, cols] + r).astype(BF)
    mask = same_patch(128, 128)
    where = [(g, h) for g in range(2) for h in range(2)]
    firsts = first_step(proj, where, mask)
    for (g, h), f in zip(where, firsts):
        m = jnp.sum(f.reshape(CHG, PAT, HD), axis=0) * (1.0 / CHG)
        agg[:, h, pl.ds(g * PAT, PAT), :] = jnp.broadcast_to(m.astype(BF)[None], (16, PAT, HD))
    for copy in copies:
        copy.wait()


def first_step(proj, where, mask):
    def part(g, h, j):
        return proj[pl.ds(g * 128, 128), pl.ds(j * 256 + h * 128, 128)]

    qs = [part(g, h, 0) for g, h in where]
    ks = [part(g, h, 1).astype(F32) for g, h in where]
    kns = [(k * inv_norm(k)).astype(BF) for k in ks]
    rqs = [inv_norm(q.astype(F32)) * FAC for q in qs]
    scores = [dot_nt(q, kn) * rq for q, kn, rq in zip(qs, kns, rqs)]
    ws = [softmax_rows(sc, mask).astype(BF) for sc in scores]
    return [dot_nn(w, part(g, h, 2)) for w, (g, h) in zip(ws, where)]


def across_kernel(proj, agg, mix_own, mix_oth, soft):
    mask = same_patch(256, 256)
    small = same_patch(128, 128)
    where = [(g, h) for h in range(2) for g in range(2)]
    seconds = []
    for h in range(2):
        q = proj[:, pl.ds(h * 128, 128)]
        rq = inv_norm(q.astype(F32))
        a = agg[:, h].reshape(256, HD)
        af = a.astype(F32)
        an = (af * inv_norm(af)).astype(BF)
        w = softmax_rows(dot_nt(q, an) * (rq * FAC), mask)
        soft[h] = w
        seconds.append(dot_nn(w.astype(BF), a))
    firsts = first_step(proj, where, small)
    for (g, h), first in zip(where, firsts):
        ref = (mix_own, mix_oth)[g]
        ref[:, pl.ds(h * 128, 128)] = (first + seconds[h][g * 128:(g + 1) * 128]).astype(BF)


def across_back_kernel(proj, agg, gm_mine, gm_got, soft, gg, gagg):
    for h in range(2):
        cols = pl.ds(h * 128, 128)
        qf = proj[:, cols].astype(F32)
        rq = inv_norm(qf)
        a = agg[:, h].reshape(256, HD)
        af = a.astype(F32)
        ra = inv_norm(af)
        an = (af * ra).astype(BF)
        w = soft[h]
        wb = w.astype(BF)
        gf = jnp.concatenate([gm_mine[:, cols], gm_got[:, cols]], 0)
        g = gf.astype(BF)
        dw = dot_nt(g, a)
        wdw = w * dw
        dsb = ((wdw - w * jnp.sum(wdw, axis=-1, keepdims=True)) * FAC).astype(BF)
        gg[:, cols] = gf
        gg[:, pl.ds(256 + h * 128, 128)] = norm_back(qf, rq, dot_nn(dsb, an))
        dan = dot_tn(dsb, (qf * rq).astype(BF))
        da = dot_tn(wb, g) + norm_back(af, ra, dan)
        gagg[:, h] = da.astype(BF).reshape(16, 16, HD)


def quarter_slots(d):
    y, x, core, z = place()
    by = (z + d) % 4
    py = slot_of((by + 4 - y) % 4)
    slots = []
    for bx in range(4):
        px = slot_of((bx + 4 - x) % 4)
        slots.append(jnp.where(core == 0, py * 4 + px, px * 4 + py))
    return slots


def fetch(wall, wv, sems, d, at):
    copies = []
    for bx, slot in enumerate(quarter_slots(d)):
        copy = pltpu.make_async_copy(wall.at[slot], wv.at[at + bx], sems.at[at + bx])
        copy.start()
        copies.append(copy)
    return copies


def block_product(stk, wv, n):
    w = jnp.concatenate([wv[n, :, j].reshape(256, 256) for j in range(3)], 1)
    return dot_nt(stk[...], w)


def back_kernel(proj, gg, ragg, wall, own, oth, stk, corr_own, corr_oth, wv, sems):
    copies = fetch(wall, wv, sems, 2, 0)
    own_grad = jnp.sum(ragg[...].astype(F32), axis=0) * (1.0 / CHG)
    mask = same_patch(128, 128)
    where = [(g, h) for g in range(2) for h in range(2)]
    fwd = [within(proj, pl.ds(g * 128, 128), h, mask) for g, h in where]
    grads = []
    for g, h in where:
        og = own_grad[h, g * PAT:(g + 1) * PAT, :]
        gf = gg[pl.ds(g * 128, 128), pl.ds(h * 128, 128)]
        grads.append((gf + jnp.broadcast_to(og[None], (CHG, PAT, HD)).reshape(128, HD)).astype(BF))
    dws = [dot_nt(gb, f[2]) for gb, f in zip(grads, fwd)]
    dvs = [dot_tn(f[6].astype(BF), gb).astype(BF) for gb, f in zip(grads, fwd)]
    dss = []
    for f, dw in zip(fwd, dws):
        wdw = f[6] * dw
        dss.append(((wdw - f[6] * jnp.sum(wdw, axis=-1, keepdims=True)) * FAC).astype(BF))
    dqs = [dot_nn(ds, f[5]) for ds, f in zip(dss, fwd)]
    dks = [dot_tn(ds, (f[0] * f[3]).astype(BF)) for ds, f in zip(dss, fwd)]
    totals = [jnp.zeros((128, 1), F32), jnp.zeros((128, 1), F32)]
    for n, (g, h) in enumerate(where):
        qf, kf, v, rq, rk, _, _ = fwd[n]
        rows = pl.ds(g * 128, 128)
        dq = (norm_back(qf, rq, dqs[n]) + gg[rows, pl.ds(256 + h * 128, 128)]).astype(BF)
        dk = norm_back(kf, rk, dks[n]).astype(BF)
        stk[rows, pl.ds(h * 128, 128)] = dq
        stk[rows, pl.ds(256 + h * 128, 128)] = dk
        stk[rows, pl.ds(512 + h * 128, 128)] = dvs[n]
        prod = dq.astype(F32) * qf + dk.astype(F32) * kf + dvs[n].astype(F32) * v.astype(F32)
        totals[g] = totals[g] + jnp.sum(prod, axis=-1, keepdims=True)
    corr_own[...] = jnp.broadcast_to(totals[0], (128, 128))
    corr_oth[...] = jnp.broadcast_to(totals[1], (128, 128))
    for copy in copies:
        copy.wait()

    def step(bx, carry):
        r = block_product(stk, wv, bx)
        cols = pl.ds(pl.multiple_of(bx * 256, 256), 256)
        own[:, cols] = r[0:128].astype(BF)
        oth[:, cols] = r[128:256].astype(BF)
        return carry

    lax.fori_loop(0, 4, step, 0)


def rest_kernel(stk, wall, own, oth, wv, sems):
    copies = []
    for n, d in enumerate((1, 3, 0)):
        copies.append(fetch(wall, wv, sems, d, n * 4))
    for n in range(3):
        for copy in copies[n]:
            copy.wait()

        def step(bx, carry):
            r = block_product(stk, wv, n * 4 + bx)
            cols = pl.ds(pl.multiple_of(bx * 256, 256), 256)
            own[n, :, cols] = r[0:128].astype(BF)
            oth[n, :, cols] = r[128:256].astype(BF)
            return carry

        lax.fori_loop(0, 4, step, 0)


def combine(mine, got, part, inv, corr_own, corr_got):
    r = inv[:, 0:1]
    c = (corr_own[:, 0:1] + corr_got[:, 0:1]) * (r * (1.0 / 4096))
    h = part[0:128, :].astype(F32)
    g = part[128:136, :].astype(F32)[0:1]
    return r * (g * (mine.astype(F32) + got.astype(F32)) - h * c)


def one_kernel(mine, got, part, inv, corr_own, corr_got, out):
    out[...] = combine(mine[...], got[...], part, inv, corr_own, corr_got).astype(BF)


def two_kernel(mine, got, part_a, part_b, inv, corr_own, corr_got, out_a, out_b):
    out_a[...] = combine(mine[0], got[0], part_a, inv, corr_own, corr_got).astype(BF)
    out_b[...] = combine(mine[1], got[1], part_b, inv, corr_own, corr_got).astype(BF)


def last_kernel(mine, got, part, inv, corr_own, corr_got, cot, r1, r2, r3, out):
    grad = combine(mine[2], got[2], part, inv, corr_own, corr_got)
    grad = grad + r1[...].astype(F32) + r2[...].astype(F32) + r3[...].astype(F32)
    out[...] = (cot[...].astype(F32) + grad).astype(BF)


def gm_kernel(c0, c1, c2, c3, ow, mine, other):
    _, _, core, z = place()
    for ref, which in ((mine, core), (other, 1 - core)):
        rows = pl.ds(pl.multiple_of(which * 256, 256), 256)
        total = jnp.zeros((128, 256), F32)
        for d, c in enumerate((c0, c1, c2, c3)):
            cols = pl.ds(pl.multiple_of(((z + 4 - d) % 4) * 1024, 1024), 1024)
            total = total + dot_nt(c[...], ow[rows, cols])
        ref[...] = total


def out_quarter(mine, got, ow, d):
    _, _, core, z = place()
    cols = pl.ds(pl.multiple_of(((z + d) % 4) * 1024, 1024), 1024)
    rows = pl.ds(pl.multiple_of(core * 256, 256), 256)
    rows_got = pl.ds(pl.multiple_of((1 - core) * 256, 256), 256)
    return dot_nn(mine[...], ow[rows, cols]) + dot_nn(got[...], ow[rows_got, cols])


def out_first_kernel(mine, got, ow, o2):
    o2[...] = out_quarter(mine, got, ow, 2).astype(BF)


def out_rest_kernel(mine, got, ow, o1, o3, o0):
    o1[...] = out_quarter(mine, got, ow, 1).astype(BF)
    o3[...] = out_quarter(mine, got, ow, 3).astype(BF)
    o0[...] = out_quarter(mine, got, ow, 0)


VM = pl.BlockSpec(memory_space=pltpu.VMEM)
AN = pl.BlockSpec(memory_space=pl.ANY)
HB = pl.BlockSpec(memory_space=pltpu.HBM)
PARAMS = pltpu.CompilerParams(vmem_limit_bytes=16 * 1024 * 1024)


def shape(dims, dtype):
    return jax.ShapeDtypeStruct(dims, dtype)


def call(kernel, ins, outs, args, scratch=()):
    return pl.pallas_call(
        kernel,
        in_specs=ins,
        out_specs=[spec for spec, _ in outs],
        out_shape=[sh for _, sh in outs],
        scratch_shapes=list(scratch),
        compiler_params=PARAMS,
    )(*args)


BLOCK = (2, 3, 128, 256)


def in_hbm(value):
    return pltpu.with_memory_space_constraint(value, pltpu.HBM)


def prepare(tokens, position, gain):
    return call(
        prepare_kernel, [HB] * 3, [(VM, shape((136, 1024), BF))],
        (in_hbm(tokens), in_hbm(position), in_hbm(gain)),
        (
            pltpu.VMEM((16, 8, 1024), BF), pltpu.VMEM((16, 1024), BF), pltpu.VMEM((1024,), BF),
            pltpu.SemaphoreType.DMA((3,)),
        ),
    )[0]


def normalise(parts):
    return call(
        norm_kernel, [VM] * 4,
        [(VM, shape((16, 128, 256), BF)), (VM, shape((128, 128), F32))], parts,
    )


WALL = pltpu.HBM((16,) + BLOCK, BF)


def project_early(own, oth, weights):
    return call(
        project_early_kernel, [VM, VM] + [VM] * 9,
        [(VM, shape((256, 768), F32)), (HB, WALL)],
        (own, oth) + weights,
        (pltpu.SemaphoreType.DMA((9,)),),
    )


def project_late(own, oth, acc, wall, weights):
    return pl.pallas_call(
        project_late_kernel,
        in_specs=[VM, VM, VM, HB] + [VM] * 6,
        out_specs=[VM, VM, HB],
        out_shape=[shape((256, 768), BF), shape((16, 2, 16, HD), BF), WALL],
        scratch_shapes=[pltpu.SemaphoreType.DMA((6,))],
        input_output_aliases={3: 2},
        compiler_params=PARAMS,
        name="late",
    )(own, oth, acc, in_hbm(wall), *weights)


def across(proj, agg):
    return call(
        across_kernel, [VM] * 2,
        [(VM, shape((128, 256), BF)), (VM, shape((128, 256), BF)), (VM, shape((2, 256, 256), F32))],
        (proj, agg),
    )


def across_back(proj, agg, gm_mine, gm_got, soft):
    return call(
        across_back_kernel, [VM] * 5,
        [(VM, shape((256, 512), F32)), (VM, shape((16, 2, 16, HD), BF))],
        (proj, agg, gm_mine, gm_got, soft),
    )


def backward(proj, gg, ragg, wall):
    return call(
        back_kernel, [VM] * 3 + [HB],
        [
            (VM, shape((128, 1024), BF)), (VM, shape((128, 1024), BF)), (VM, shape((256, 768), BF)),
            (VM, shape((128, 128), F32)), (VM, shape((128, 128), F32)),
        ],
        (proj, gg, ragg, in_hbm(wall)),
        (pltpu.VMEM((4,) + BLOCK, BF), pltpu.SemaphoreType.DMA((4,))),
    )


def rest(stk, wall):
    return call(
        rest_kernel, [VM, HB],
        [(VM, shape((3, 128, 1024), BF)), (VM, shape((3, 128, 1024), BF))],
        (stk, in_hbm(wall)),
        (pltpu.VMEM((12,) + BLOCK, BF), pltpu.SemaphoreType.DMA((12,))),
    )


def own_weights(qkv_weight, core):
    mine = lax.dynamic_slice_in_dim(qkv_weight, core * 256, 256, 2)
    other = lax.dynamic_slice_in_dim(qkv_weight, (1 - core) * 256, 256, 2)
    got = swap(other)
    lead = core == 0
    return jnp.stack([jnp.where(lead, mine, got), jnp.where(lead, got, mine)])


def gather_weights(own):
    def near(value, step):
        return lax.ppermute(value, "chan", ring(True, step))

    def cross(value, step):
        return lax.ppermute(value, "chan", ring(False, step))

    r = near(own, 1)
    l = near(own, -1)

    up = cross(own, 1)
    down = cross(own, -1)
    pair = jnp.stack([r, l])
    far = jnp.concatenate([near(r[:1], 1), near(l[1:], -1)], 0)
    pair_up = cross(pair, 1)
    pair_down = cross(pair, -1)
    over_a = cross(up[:1], 1)
    over_b = cross(down[1:], -1)
    far_up = cross(far, 1)
    far_down = cross(far, -1)
    pair_a = cross(pair_up[0], 1)
    pair_b = cross(pair_down[1], -1)
    far_a = cross(far_up[:1], 1)
    far_b = cross(far_down[1:], -1)

    def whole(value):
        return value.reshape((-1,) + value.shape[-4:])

    lead = tuple(whole(v) for v in (own, pair, far, up, down, pair_up, pair_down, far_up, far_down))
    tail = (over_a, over_b, whole(pair_a), whole(pair_b), far_a, far_b)
    return lead, tail, far


def layer(tokens, position, gain, qkv_weight, out_weight, cotangent):
    _, _, core, _ = place()

    own_w = own_weights(qkv_weight, core)
    message = prepare(tokens, position, gain)
    h_parts = [message]
    for d in (1, 2, 3):
        h_parts.append(zshift(message, d))
    early, late, far = gather_weights(own_w)

    waited, _ = lax.optimization_barrier((h_parts, far))
    normed, inv_rms = normalise(waited)
    cot = cotangent.reshape(128, 1024)
    cot_b, normed = lax.optimization_barrier((cot, normed))
    c_parts = [cot_b]
    for d in (1, 2, 3):
        c_parts.append(zshift(cot_b, d))
    normed_other = swap(normed)
    acc, wall = project_early(normed, normed_other, early)
    proj, agg, wall = project_late(normed, normed_other, acc, wall, late)
    agg_all = lax.all_to_all(agg, "chan", 0, 0, axis_index_groups=SAME_CORE, tiled=True)

    gm_mine, gm_other = call(
        gm_kernel, [VM] * 5, [(VM, shape((128, 256), F32))] * 2, c_parts + [out_weight],
    )
    gm_got = swap(gm_other)

    mix_own, mix_oth, soft = across(proj, agg_all)
    mix_got = swap(mix_oth)
    gg, gagg = across_back(proj, agg_all, gm_mine, gm_got, soft)
    ragg = lax.all_to_all(gagg, "chan", 0, 0, axis_index_groups=SAME_CORE, tiled=True)

    o2, = call(
        out_first_kernel, [VM] * 3, [(VM, shape((128, 1024), BF))], (mix_own, mix_got, out_weight),
    )
    s2 = zshift(o2, 2)
    o1, o3, o0 = call(
        out_rest_kernel, [VM] * 3,
        [(VM, shape((128, 1024), BF)), (VM, shape((128, 1024), BF)), (VM, shape((128, 1024), F32))],
        (mix_own, mix_got, out_weight),
    )
    s1 = zshift(o1, 1)
    s3 = zshift(o3, 3)
    summed = o0 + s1.astype(F32) + s2.astype(F32) + s3.astype(F32)
    layer_out = (summed + message[:128].astype(F32)).astype(BF)

    own2, oth2, stk, corr_own, corr_oth = backward(proj, gg, ragg, wall)
    got2 = swap(oth2)
    corr_got = swap(corr_oth)
    own_r, oth_r = rest(stk, wall)
    got_r = swap(oth_r)
    scal = (inv_rms, corr_own, corr_got)
    msg2, = call(one_kernel, [VM] * 6, [(VM, shape((128, 1024), BF))], (own2, got2, h_parts[2]) + scal)
    r2 = zshift(msg2, 2)
    msg1, msg3 = call(
        two_kernel, [VM] * 7, [(VM, shape((128, 1024), BF))] * 2,
        (own_r, got_r, h_parts[3], h_parts[1]) + scal,
    )
    r1 = zshift(msg1, 1)
    r3 = zshift(msg3, 3)
    input_grad, = call(
        last_kernel, [VM] * 10, [(VM, shape((128, 1024), BF))],
        (own_r, got_r, h_parts[0]) + scal + (cot, r1, r2, r3),
    )
    return layer_out.reshape(16, 8, 1024), input_grad.reshape(16, 8, 1024)


def solution(mesh):
    return jax.shard_map(
        layer,
        mesh=mesh,
        in_specs=(
            P("chan", "region", "head"),
            P("chan", "head"),
            P("head"),
            P(None, "chan", "head"),
            P("head", None),
            P("chan", "region", "head"),
        ),
        out_specs=(P("chan", "region", "head"), P("chan", "region", "head")),
        check_vma=False,
    )
```

```python
import jax
import jax.numpy as jnp
from jax import lax
from jax.experimental import pallas as pl
from jax.experimental.pallas import tpu as pltpu
from jax.sharding import PartitionSpec as P


F32 = jnp.float32
BF = jnp.bfloat16
NY, NX, NC, NZ = 4, 4, 2, 4
HD = 128
FAC = HD ** -0.5
CHG = 16
PAT = 8


def chan_id(y, x, c):
    return (y % NY) * (NX * NC) + (x % NX) * NC + (c % NC)


SITES = [(y, x, c) for y in range(NY) for x in range(NX) for c in range(NC)]
SWAP = [(chan_id(y, x, c), chan_id(y, x, c + 1)) for y, x, c in SITES]
SAME_CORE = [[chan_id(y, x, c) for y in range(NY) for x in range(NX)] for c in range(NC)]


def ring(first, step):
    pairs = []
    for y, x, c in SITES:
        if (c == 0) == first:
            pairs.append((chan_id(y, x, c), chan_id(y, x + step, c)))
        else:
            pairs.append((chan_id(y, x, c), chan_id(y + step, x, c)))
    return pairs


def swap(value):
    return lax.ppermute(value, "chan", SWAP)


def zshift(value, step):
    return lax.ppermute(value, "head", [(i, (i + step) % NZ) for i in range(NZ)])


def dot_nt(a, b):
    return lax.dot_general(a, b, (((1,), (1,)), ((), ())), preferred_element_type=F32)


def dot_nn(a, b):
    return lax.dot_general(a, b, (((1,), (0,)), ((), ())), preferred_element_type=F32)


def dot_tn(a, b):
    return lax.dot_general(a, b, (((0,), (0,)), ((), ())), preferred_element_type=F32)


def inv_norm(u):
    return lax.rsqrt(jnp.mean(u * u, axis=-1, keepdims=True) + 1e-06)


def norm_back(u, r, dy):
    return r * dy - u * (r * r * r * jnp.mean(dy * u, axis=-1, keepdims=True))


def same_patch(rows, cols):
    ri = lax.broadcasted_iota(jnp.int32, (rows, cols), 0) % PAT
    ci = lax.broadcasted_iota(jnp.int32, (rows, cols), 1) % PAT
    return ri == ci


def softmax_rows(scores, mask):
    e = jnp.where(mask, jnp.exp(scores), 0.0)
    return e * (1.0 / jnp.sum(e, axis=-1, keepdims=True))


def place():
    chan = lax.axis_index("chan")
    return chan // 8, (chan // 2) % 4, chan % 2, lax.axis_index("head")


def slot_of(off):
    return jnp.where(off == 3, 1, jnp.where(off == 1, 2, jnp.where(off == 2, 3, 0)))


def within(proj, rows, h, mask):
    q = proj[rows, pl.ds(h * 128, 128)]
    k = proj[rows, pl.ds(256 + h * 128, 128)]
    v = proj[rows, pl.ds(512 + h * 128, 128)]
    qf = q.astype(F32)
    kf = k.astype(F32)
    rq = inv_norm(qf)
    rk = inv_norm(kf)
    kn = (kf * rk).astype(BF)
    w = softmax_rows(dot_nt(q, kn) * (rq * FAC), mask)
    return qf, kf, v, rq, rk, kn, w


def prepare_kernel(tokens, position, gain, message, tok, pos, gn, sems):
    copies = [
        pltpu.make_async_copy(tokens, tok, sems.at[0]),
        pltpu.make_async_copy(position, pos, sems.at[1]),
        pltpu.make_async_copy(gain, gn, sems.at[2]),
    ]
    for copy in copies:
        copy.start()
    for copy in copies:
        copy.wait()
    hidden = tok[...].astype(F32) + pos[...].astype(F32)[:, None, :]
    message[0:128, :] = hidden.reshape(128, 1024).astype(BF)
    message[128:136, :] = jnp.broadcast_to(gn[...][None], (8, 1024))


def norm_kernel(p0, p1, p2, p3, normed, inv):
    parts = (p0, p1, p2, p3)
    square = jnp.zeros((128, 1), F32)
    for p in parts:
        h = p[0:128, :].astype(F32)
        square = square + jnp.sum(h * h, axis=-1, keepdims=True)
    r = lax.rsqrt(square * (1.0 / 4096) + 1e-05)
    inv[...] = jnp.broadcast_to(r, (128, 128))
    for n, p in enumerate(parts):
        for b in range(4):
            cols = pl.ds(b * 256, 256)
            h = p[0:128, cols].astype(F32)
            g = p[128:136, cols].astype(F32)[0:1]
            normed[n * 4 + b] = (h * r * g).astype(BF)


EARLY = ((0, 1), (1, 2), (3, 1), (4, 1), (8, 1), (5, 2), (9, 2), (7, 1), (11, 1))
LATE = ((0, "a"), (0, "b"), (1, 1), (2, 1), (3, "a"), (3, "b"))


def save_pieces(pieces, places, wall, base, sems):
    copies = []
    for n, (ref, (slot, size)) in enumerate(zip(pieces, places)):
        if size == "a":
            dst = wall.at[base + slot, 0:1]
        elif size == "b":
            dst = wall.at[base + slot, 1:2]
        else:
            dst = wall.at[base + slot:base + slot + size]
        copy = pltpu.make_async_copy(ref, dst, sems.at[n])
        copy.start()
        copies.append(copy)
    return copies


def rows_of(pieces, j):
    parts = []
    for ref in pieces:
        if len(ref.shape) == 4:
            parts.append(ref[0, j])
        else:
            parts.append(ref[:, :, j].reshape(-1, 256))
    return jnp.concatenate(parts, 0)


def group_lhs(own, oth, s3):
    y, x, core, z = place()
    lead = core == 0
    parts = []
    for s1 in (0, 3, 1, 2):
        by = (y + jnp.where(lead, s3, s1)) % 4
        bx = (x + jnp.where(lead, s1, s3)) % 4
        blk = ((z + 4 - by) % 4) * 4 + bx
        parts.append(jnp.concatenate([own[blk], oth[blk]], 0))
    return jnp.concatenate(parts, 1)


def project_early_kernel(own, oth, *refs):
    pieces = refs[:9]
    acc, wall, sems = refs[9:]
    copies = save_pieces(pieces, EARLY, wall, 0, sems)
    for n, group in enumerate(((0, 1, 2), (3, 5, 7), (4, 6, 8))):
        lhs = group_lhs(own, oth, (0, 3, 1)[n])
        for j in range(3):
            cols = slice(j * 256, (j + 1) * 256)
            r = dot_nn(lhs, rows_of([pieces[at] for at in group], j))
            if n == 0:
                acc[:, cols] = r
            else:
                acc[:, cols] += r
    for copy in copies:
        copy.wait()


def project_late_kernel(own, oth, acc, wall_in, *refs):
    pieces = refs[:6]
    proj, agg, wall, sems = refs[6:]
    copies = save_pieces(pieces, LATE, wall, 12, sems)
    lhs = group_lhs(own, oth, 2)
    for j in range(3):
        cols = slice(j * 256, (j + 1) * 256)
        r = dot_nn(lhs, rows_of(pieces, j))
        proj[:, cols] = (acc[:, cols] + r).astype(BF)
    mask = same_patch(128, 128)
    where = [(g, h) for g in range(2) for h in range(2)]
    firsts = first_step(proj, where, mask)
    for (g, h), f in zip(where, firsts):
        m = jnp.sum(f.reshape(CHG, PAT, HD), axis=0) * (1.0 / CHG)
        agg[:, h, pl.ds(g * PAT, PAT), :] = jnp.broadcast_to(m.astype(BF)[None], (16, PAT, HD))
    for copy in copies:
        copy.wait()


def first_step(proj, where, mask):
    def part(g, h, j):
        return proj[pl.ds(g * 128, 128), pl.ds(j * 256 + h * 128, 128)]

    qs = [part(g, h, 0) for g, h in where]
    ks = [part(g, h, 1).astype(F32) for g, h in where]
    kns = [(k * inv_norm(k)).astype(BF) for k in ks]
    rqs = [inv_norm(q.astype(F32)) * FAC for q in qs]
    scores = [dot_nt(q, kn) * rq for q, kn, rq in zip(qs, kns, rqs)]
    ws = [softmax_rows(sc, mask).astype(BF) for sc in scores]
    return [dot_nn(w, part(g, h, 2)) for w, (g, h) in zip(ws, where)]


def across_kernel(proj, agg, mix_own, mix_oth, soft):
    mask = same_patch(256, 256)
    small = same_patch(128, 128)
    where = [(g, h) for h in range(2) for g in range(2)]
    seconds = []
    for h in range(2):
        q = proj[:, pl.ds(h * 128, 128)]
        rq = inv_norm(q.astype(F32))
        a = agg[:, h].reshape(256, HD)
        af = a.astype(F32)
        an = (af * inv_norm(af)).astype(BF)
        w = softmax_rows(dot_nt(q, an) * (rq * FAC), mask)
        soft[h] = w
        seconds.append(dot_nn(w.astype(BF), a))
    firsts = first_step(proj, where, small)
    for (g, h), first in zip(where, firsts):
        ref = (mix_own, mix_oth)[g]
        ref[:, pl.ds(h * 128, 128)] = (first + seconds[h][g * 128:(g + 1) * 128]).astype(BF)


def across_back_kernel(proj, agg, gm_mine, gm_got, soft, gg, gagg):
    for h in range(2):
        cols = pl.ds(h * 128, 128)
        qf = proj[:, cols].astype(F32)
        rq = inv_norm(qf)
        a = agg[:, h].reshape(256, HD)
        af = a.astype(F32)
        ra = inv_norm(af)
        an = (af * ra).astype(BF)
        w = soft[h]
        wb = w.astype(BF)
        gf = jnp.concatenate([gm_mine[:, cols], gm_got[:, cols]], 0)
        g = gf.astype(BF)
        dw = dot_nt(g, a)
        wdw = w * dw
        dsb = ((wdw - w * jnp.sum(wdw, axis=-1, keepdims=True)) * FAC).astype(BF)
        gg[:, cols] = gf
        gg[:, pl.ds(256 + h * 128, 128)] = norm_back(qf, rq, dot_nn(dsb, an))
        dan = dot_tn(dsb, (qf * rq).astype(BF))
        da = dot_tn(wb, g) + norm_back(af, ra, dan)
        gagg[:, h] = da.astype(BF).reshape(16, 16, HD)


def quarter_slots(d):
    y, x, core, z = place()
    by = (z + d) % 4
    py = slot_of((by + 4 - y) % 4)
    slots = []
    for bx in range(4):
        px = slot_of((bx + 4 - x) % 4)
        slots.append(jnp.where(core == 0, py * 4 + px, px * 4 + py))
    return slots


def fetch(wall, wv, sems, d, at):
    copies = []
    for bx, slot in enumerate(quarter_slots(d)):
        copy = pltpu.make_async_copy(wall.at[slot], wv.at[at + bx], sems.at[at + bx])
        copy.start()
        copies.append(copy)
    return copies


def block_product(stk, wv, n):
    w = jnp.concatenate([wv[n, :, j].reshape(256, 256) for j in range(3)], 1)
    return dot_nt(stk[...], w)


def back_kernel(proj, gg, ragg, wall, own, oth, stk, corr_own, corr_oth, wv, sems):
    copies = fetch(wall, wv, sems, 2, 0)
    own_grad = jnp.sum(ragg[...].astype(F32), axis=0) * (1.0 / CHG)
    mask = same_patch(128, 128)
    where = [(g, h) for g in range(2) for h in range(2)]
    fwd = [within(proj, pl.ds(g * 128, 128), h, mask) for g, h in where]
    grads = []
    for g, h in where:
        og = own_grad[h, g * PAT:(g + 1) * PAT, :]
        gf = gg[pl.ds(g * 128, 128), pl.ds(h * 128, 128)]
        grads.append((gf + jnp.broadcast_to(og[None], (CHG, PAT, HD)).reshape(128, HD)).astype(BF))
    dws = [dot_nt(gb, f[2]) for gb, f in zip(grads, fwd)]
    dvs = [dot_tn(f[6].astype(BF), gb).astype(BF) for gb, f in zip(grads, fwd)]
    dss = []
    for f, dw in zip(fwd, dws):
        wdw = f[6] * dw
        dss.append(((wdw - f[6] * jnp.sum(wdw, axis=-1, keepdims=True)) * FAC).astype(BF))
    dqs = [dot_nn(ds, f[5]) for ds, f in zip(dss, fwd)]
    dks = [dot_tn(ds, (f[0] * f[3]).astype(BF)) for ds, f in zip(dss, fwd)]
    totals = [jnp.zeros((128, 1), F32), jnp.zeros((128, 1), F32)]
    for n, (g, h) in enumerate(where):
        qf, kf, v, rq, rk, _, _ = fwd[n]
        rows = pl.ds(g * 128, 128)
        dq = (norm_back(qf, rq, dqs[n]) + gg[rows, pl.ds(256 + h * 128, 128)]).astype(BF)
        dk = norm_back(kf, rk, dks[n]).astype(BF)
        stk[rows, pl.ds(h * 128, 128)] = dq
        stk[rows, pl.ds(256 + h * 128, 128)] = dk
        stk[rows, pl.ds(512 + h * 128, 128)] = dvs[n]
        prod = dq.astype(F32) * qf + dk.astype(F32) * kf + dvs[n].astype(F32) * v.astype(F32)
        totals[g] = totals[g] + jnp.sum(prod, axis=-1, keepdims=True)
    corr_own[...] = jnp.broadcast_to(totals[0], (128, 128))
    corr_oth[...] = jnp.broadcast_to(totals[1], (128, 128))
    for copy in copies:
        copy.wait()

    def step(bx, carry):
        r = block_product(stk, wv, bx)
        cols = pl.ds(pl.multiple_of(bx * 256, 256), 256)
        own[:, cols] = r[0:128].astype(BF)
        oth[:, cols] = r[128:256].astype(BF)
        return carry

    lax.fori_loop(0, 4, step, 0)


def side_kernel(stk, wall, own, oth, wv, sems):
    copies = []
    for n, d in enumerate((1, 3)):
        copies.append(fetch(wall, wv, sems, d, n * 4))
    for n in range(2):
        for copy in copies[n]:
            copy.wait()

        def step(bx, carry):
            r = block_product(stk, wv, n * 4 + bx)
            cols = pl.ds(pl.multiple_of(bx * 256, 256), 256)
            own[n, :, cols] = r[0:128].astype(BF)
            oth[n, :, cols] = r[128:256].astype(BF)
            return carry

        lax.fori_loop(0, 4, step, 0)


def home_kernel(stk, wall, own, oth, wv, sems):
    for copy in fetch(wall, wv, sems, 0, 0):
        copy.wait()

    def step(bx, carry):
        r = block_product(stk, wv, bx)
        cols = pl.ds(pl.multiple_of(bx * 256, 256), 256)
        own[:, cols] = r[0:128].astype(BF)
        oth[:, cols] = r[128:256].astype(BF)
        return carry

    lax.fori_loop(0, 4, step, 0)


def combine(mine, got, part, inv, corr_own, corr_got):
    r = inv[:, 0:1]
    c = (corr_own[:, 0:1] + corr_got[:, 0:1]) * (r * (1.0 / 4096))
    h = part[0:128, :].astype(F32)
    g = part[128:136, :].astype(F32)[0:1]
    return r * (g * (mine.astype(F32) + got.astype(F32)) - h * c)


def one_kernel(mine, got, part, inv, corr_own, corr_got, out):
    out[...] = combine(mine[...], got[...], part, inv, corr_own, corr_got).astype(BF)


def two_kernel(mine, got, part_a, part_b, inv, corr_own, corr_got, out_a, out_b):
    out_a[...] = combine(mine[0], got[0], part_a, inv, corr_own, corr_got).astype(BF)
    out_b[...] = combine(mine[1], got[1], part_b, inv, corr_own, corr_got).astype(BF)


def last_kernel(mine, got, part, inv, corr_own, corr_got, cot, r1, r2, r3, out):
    grad = combine(mine[...], got[...], part, inv, corr_own, corr_got)
    grad = grad + r1[...].astype(F32) + r2[...].astype(F32) + r3[...].astype(F32)
    out[...] = (cot[...].astype(F32) + grad).astype(BF)


def gm_kernel(c0, c1, c2, c3, ow, mine, other):
    _, _, core, z = place()
    for ref, which in ((mine, core), (other, 1 - core)):
        rows = pl.ds(pl.multiple_of(which * 256, 256), 256)
        total = jnp.zeros((128, 256), F32)
        for d, c in enumerate((c0, c1, c2, c3)):
            cols = pl.ds(pl.multiple_of(((z + 4 - d) % 4) * 1024, 1024), 1024)
            total = total + dot_nt(c[...], ow[rows, cols])
        ref[...] = total


def out_quarter(mine, got, ow, d):
    _, _, core, z = place()
    cols = pl.ds(pl.multiple_of(((z + d) % 4) * 1024, 1024), 1024)
    rows = pl.ds(pl.multiple_of(core * 256, 256), 256)
    rows_got = pl.ds(pl.multiple_of((1 - core) * 256, 256), 256)
    return dot_nn(mine[...], ow[rows, cols]) + dot_nn(got[...], ow[rows_got, cols])


def out_first_kernel(mine, got, ow, o2):
    o2[...] = out_quarter(mine, got, ow, 2).astype(BF)


def out_rest_kernel(mine, got, ow, o1, o3, o0):
    o1[...] = out_quarter(mine, got, ow, 1).astype(BF)
    o3[...] = out_quarter(mine, got, ow, 3).astype(BF)
    o0[...] = out_quarter(mine, got, ow, 0)


VM = pl.BlockSpec(memory_space=pltpu.VMEM)
AN = pl.BlockSpec(memory_space=pl.ANY)
HB = pl.BlockSpec(memory_space=pltpu.HBM)
PARAMS = pltpu.CompilerParams(vmem_limit_bytes=16 * 1024 * 1024)


def shape(dims, dtype):
    return jax.ShapeDtypeStruct(dims, dtype)


def call(kernel, ins, outs, args, scratch=()):
    return pl.pallas_call(
        kernel,
        in_specs=ins,
        out_specs=[spec for spec, _ in outs],
        out_shape=[sh for _, sh in outs],
        scratch_shapes=list(scratch),
        compiler_params=PARAMS,
    )(*args)


BLOCK = (2, 3, 128, 256)


def in_hbm(value):
    return pltpu.with_memory_space_constraint(value, pltpu.HBM)


def prepare(tokens, position, gain):
    return call(
        prepare_kernel, [HB] * 3, [(VM, shape((136, 1024), BF))],
        (in_hbm(tokens), in_hbm(position), in_hbm(gain)),
        (
            pltpu.VMEM((16, 8, 1024), BF), pltpu.VMEM((16, 1024), BF), pltpu.VMEM((1024,), BF),
            pltpu.SemaphoreType.DMA((3,)),
        ),
    )[0]


def normalise(parts):
    return call(
        norm_kernel, [VM] * 4,
        [(VM, shape((16, 128, 256), BF)), (VM, shape((128, 128), F32))], parts,
    )


WALL = pltpu.HBM((16,) + BLOCK, BF)


def project_early(own, oth, weights):
    return call(
        project_early_kernel, [VM, VM] + [VM] * 9,
        [(VM, shape((256, 768), F32)), (HB, WALL)],
        (own, oth) + weights,
        (pltpu.SemaphoreType.DMA((9,)),),
    )


def project_late(own, oth, acc, wall, weights):
    return pl.pallas_call(
        project_late_kernel,
        in_specs=[VM, VM, VM, HB] + [VM] * 6,
        out_specs=[VM, VM, HB],
        out_shape=[shape((256, 768), BF), shape((16, 2, 16, HD), BF), WALL],
        scratch_shapes=[pltpu.SemaphoreType.DMA((6,))],
        input_output_aliases={3: 2},
        compiler_params=PARAMS,
        name="late",
    )(own, oth, acc, in_hbm(wall), *weights)


def across(proj, agg):
    return call(
        across_kernel, [VM] * 2,
        [(VM, shape((128, 256), BF)), (VM, shape((128, 256), BF)), (VM, shape((2, 256, 256), F32))],
        (proj, agg),
    )


def across_back(proj, agg, gm_mine, gm_got, soft):
    return call(
        across_back_kernel, [VM] * 5,
        [(VM, shape((256, 512), F32)), (VM, shape((16, 2, 16, HD), BF))],
        (proj, agg, gm_mine, gm_got, soft),
    )


def backward(proj, gg, ragg, wall):
    return call(
        back_kernel, [VM] * 3 + [HB],
        [
            (VM, shape((128, 1024), BF)), (VM, shape((128, 1024), BF)), (VM, shape((256, 768), BF)),
            (VM, shape((128, 128), F32)), (VM, shape((128, 128), F32)),
        ],
        (proj, gg, ragg, in_hbm(wall)),
        (pltpu.VMEM((4,) + BLOCK, BF), pltpu.SemaphoreType.DMA((4,))),
    )


def side(stk, wall):
    return call(
        side_kernel, [VM, HB], [(VM, shape((2, 128, 1024), BF))] * 2, (stk, in_hbm(wall)),
        (pltpu.VMEM((8,) + BLOCK, BF), pltpu.SemaphoreType.DMA((8,))),
    )


def home(stk, wall):
    return call(
        home_kernel, [VM, HB], [(VM, shape((128, 1024), BF))] * 2, (stk, in_hbm(wall)),
        (pltpu.VMEM((4,) + BLOCK, BF), pltpu.SemaphoreType.DMA((4,))),
    )


def own_weights(qkv_weight, core):
    mine = lax.dynamic_slice_in_dim(qkv_weight, core * 256, 256, 2)
    other = lax.dynamic_slice_in_dim(qkv_weight, (1 - core) * 256, 256, 2)
    got = swap(other)
    lead = core == 0
    return jnp.stack([jnp.where(lead, mine, got), jnp.where(lead, got, mine)])


def gather_weights(own):
    def near(value, step):
        return lax.ppermute(value, "chan", ring(True, step))

    def cross(value, step):
        return lax.ppermute(value, "chan", ring(False, step))

    r = near(own, 1)
    l = near(own, -1)

    up = cross(own, 1)
    down = cross(own, -1)
    pair = jnp.stack([r, l])
    far = jnp.concatenate([near(r[:1], 1), near(l[1:], -1)], 0)
    pair_up = cross(pair, 1)
    pair_down = cross(pair, -1)
    over_a = cross(up[:1], 1)
    over_b = cross(down[1:], -1)
    far_up = cross(far, 1)
    far_down = cross(far, -1)
    pair_a = cross(pair_up[0], 1)
    pair_b = cross(pair_down[1], -1)
    far_a = cross(far_up[:1], 1)
    far_b = cross(far_down[1:], -1)

    def whole(value):
        return value.reshape((-1,) + value.shape[-4:])

    lead = tuple(whole(v) for v in (own, pair, far, up, down, pair_up, pair_down, far_up, far_down))
    tail = (over_a, over_b, whole(pair_a), whole(pair_b), far_a, far_b)
    return lead, tail, far


def layer(tokens, position, gain, qkv_weight, out_weight, cotangent):
    _, _, core, _ = place()

    own_w = own_weights(qkv_weight, core)
    message = prepare(tokens, position, gain)
    h_parts = [message]
    for d in (1, 2, 3):
        h_parts.append(zshift(message, d))
    early, late, far = gather_weights(own_w)

    waited, _ = lax.optimization_barrier((h_parts, far))
    normed, inv_rms = normalise(waited)
    cot = cotangent.reshape(128, 1024)
    c_parts = [cot]
    for d in (1, 2, 3):
        c_parts.append(zshift(cot, d))
    normed_other = swap(normed)
    acc, wall = project_early(normed, normed_other, early)
    proj, agg, wall = project_late(normed, normed_other, acc, wall, late)
    agg_all = lax.all_to_all(agg, "chan", 0, 0, axis_index_groups=SAME_CORE, tiled=True)

    gm_mine, gm_other = call(
        gm_kernel, [VM] * 5, [(VM, shape((128, 256), F32))] * 2, c_parts + [out_weight],
    )
    gm_got = swap(gm_other)

    mix_own, mix_oth, soft = across(proj, agg_all)
    mix_got = swap(mix_oth)
    gg, gagg = across_back(proj, agg_all, gm_mine, gm_got, soft)
    ragg = lax.all_to_all(gagg, "chan", 0, 0, axis_index_groups=SAME_CORE, tiled=True)

    o2, = call(
        out_first_kernel, [VM] * 3, [(VM, shape((128, 1024), BF))], (mix_own, mix_got, out_weight),
    )
    s2 = zshift(o2, 2)
    o1, o3, o0 = call(
        out_rest_kernel, [VM] * 3,
        [(VM, shape((128, 1024), BF)), (VM, shape((128, 1024), BF)), (VM, shape((128, 1024), F32))],
        (mix_own, mix_got, out_weight),
    )
    s1 = zshift(o1, 1)
    s3 = zshift(o3, 3)
    summed = o0 + s1.astype(F32) + s2.astype(F32) + s3.astype(F32)
    layer_out = (summed + message[:128].astype(F32)).astype(BF)

    own2, oth2, stk, corr_own, corr_oth = backward(proj, gg, ragg, wall)
    got2 = swap(oth2)
    corr_got = swap(corr_oth)
    own_r, oth_r = side(stk, wall)
    got_r = swap(oth_r)
    scal = (inv_rms, corr_own, corr_got)
    msg2, = call(one_kernel, [VM] * 6, [(VM, shape((128, 1024), BF))], (own2, got2, h_parts[2]) + scal)
    r2 = zshift(msg2, 2)
    msg1, msg3 = call(
        two_kernel, [VM] * 7, [(VM, shape((128, 1024), BF))] * 2,
        (own_r, got_r, h_parts[3], h_parts[1]) + scal,
    )
    r1 = zshift(msg1, 1)
    r3 = zshift(msg3, 3)
    own_h, oth_h = home(stk, wall)
    got_h = swap(oth_h)
    input_grad, = call(
        last_kernel, [VM] * 10, [(VM, shape((128, 1024), BF))],
        (own_h, got_h, h_parts[0]) + scal + (cot, r1, r2, r3),
    )
    return layer_out.reshape(16, 8, 1024), input_grad.reshape(16, 8, 1024)


def solution(mesh):
    return jax.shard_map(
        layer,
        mesh=mesh,
        in_specs=(
            P("chan", "region", "head"),
            P("chan", "head"),
            P("head"),
            P(None, "chan", "head"),
            P("head", None),
            P("chan", "region", "head"),
        ),
        out_specs=(P("chan", "region", "head"), P("chan", "region", "head")),
        check_vma=False,
    )
```

```python
import jax
import jax.numpy as jnp
from jax import lax
from jax.experimental import pallas as pl
from jax.experimental.pallas import tpu as pltpu
from jax.sharding import PartitionSpec as P


F32 = jnp.float32
BF = jnp.bfloat16
NY, NX, NC, NZ = 4, 4, 2, 4
HD = 128
FAC = HD ** -0.5
CHG = 16
PAT = 8


def chan_id(y, x, c):
    return (y % NY) * (NX * NC) + (x % NX) * NC + (c % NC)


SITES = [(y, x, c) for y in range(NY) for x in range(NX) for c in range(NC)]
SWAP = [(chan_id(y, x, c), chan_id(y, x, c + 1)) for y, x, c in SITES]
SAME_CORE = [[chan_id(y, x, c) for y in range(NY) for x in range(NX)] for c in range(NC)]


def ring(first, step):
    pairs = []
    for y, x, c in SITES:
        if (c == 0) == first:
            pairs.append((chan_id(y, x, c), chan_id(y, x + step, c)))
        else:
            pairs.append((chan_id(y, x, c), chan_id(y + step, x, c)))
    return pairs


def swap(value):
    return lax.ppermute(value, "chan", SWAP)


def zshift(value, step):
    return lax.ppermute(value, "head", [(i, (i + step) % NZ) for i in range(NZ)])


def dot_nt(a, b):
    return lax.dot_general(a, b, (((1,), (1,)), ((), ())), preferred_element_type=F32)


def dot_nn(a, b):
    return lax.dot_general(a, b, (((1,), (0,)), ((), ())), preferred_element_type=F32)


def dot_tn(a, b):
    return lax.dot_general(a, b, (((0,), (0,)), ((), ())), preferred_element_type=F32)


def inv_norm(u):
    return lax.rsqrt(jnp.mean(u * u, axis=-1, keepdims=True) + 1e-06)


def norm_back(u, r, dy):
    return r * dy - u * (r * r * r * jnp.mean(dy * u, axis=-1, keepdims=True))


def same_patch(rows, cols):
    ri = lax.broadcasted_iota(jnp.int32, (rows, cols), 0) % PAT
    ci = lax.broadcasted_iota(jnp.int32, (rows, cols), 1) % PAT
    return ri == ci


def softmax_rows(scores, mask):
    e = jnp.where(mask, jnp.exp(scores), 0.0)
    return e * (1.0 / jnp.sum(e, axis=-1, keepdims=True))


def place():
    chan = lax.axis_index("chan")
    return chan // 8, (chan // 2) % 4, chan % 2, lax.axis_index("head")


def slot_of(off):
    return jnp.where(off == 3, 1, jnp.where(off == 1, 2, jnp.where(off == 2, 3, 0)))


def within(proj, rows, h, mask):
    q = proj[rows, pl.ds(h * 128, 128)]
    k = proj[rows, pl.ds(256 + h * 128, 128)]
    v = proj[rows, pl.ds(512 + h * 128, 128)]
    qf = q.astype(F32)
    kf = k.astype(F32)
    rq = inv_norm(qf)
    rk = inv_norm(kf)
    kn = (kf * rk).astype(BF)
    w = softmax_rows(dot_nt(q, kn) * (rq * FAC), mask)
    return qf, kf, v, rq, rk, kn, w


def prepare_kernel(tokens, position, gain, message, tok, pos, gn, sems):
    copies = [
        pltpu.make_async_copy(tokens, tok, sems.at[0]),
        pltpu.make_async_copy(position, pos, sems.at[1]),
        pltpu.make_async_copy(gain, gn, sems.at[2]),
    ]
    for copy in copies:
        copy.start()
    for copy in copies:
        copy.wait()
    hidden = tok[...].astype(F32) + pos[...].astype(F32)[:, None, :]
    message[0:128, :] = hidden.reshape(128, 1024).astype(BF)
    message[128:136, :] = jnp.broadcast_to(gn[...][None], (8, 1024))


def norm_kernel(p0, p1, p2, p3, normed, inv):
    parts = (p0, p1, p2, p3)
    square = jnp.zeros((128, 1), F32)
    for p in parts:
        h = p[0:128, :].astype(F32)
        square = square + jnp.sum(h * h, axis=-1, keepdims=True)
    r = lax.rsqrt(square * (1.0 / 4096) + 1e-05)
    inv[...] = jnp.broadcast_to(r, (128, 128))
    for n, p in enumerate(parts):
        for b in range(4):
            cols = pl.ds(b * 256, 256)
            h = p[0:128, cols].astype(F32)
            g = p[128:136, cols].astype(F32)[0:1]
            normed[n * 4 + b] = (h * r * g).astype(BF)


EARLY = ((0, 1), (1, 2), (3, 1), (4, 1), (8, 1), (5, 2), (9, 2), (7, 1), (11, 1))
LATE = ((0, "a"), (0, "b"), (1, 1), (2, 1), (3, "a"), (3, "b"))


def save_pieces(pieces, places, wall, base, sems):
    copies = []
    for n, (ref, (slot, size)) in enumerate(zip(pieces, places)):
        if size == "a":
            dst = wall.at[base + slot, 0:1]
        elif size == "b":
            dst = wall.at[base + slot, 1:2]
        else:
            dst = wall.at[base + slot:base + slot + size]
        copy = pltpu.make_async_copy(ref, dst, sems.at[n])
        copy.start()
        copies.append(copy)
    return copies


def rows_of(pieces, j):
    parts = []
    for ref in pieces:
        if len(ref.shape) == 4:
            parts.append(ref[0, j])
        else:
            parts.append(ref[:, :, j].reshape(-1, 256))
    return jnp.concatenate(parts, 0)


def group_lhs(own, oth, s3):
    y, x, core, z = place()
    lead = core == 0
    parts = []
    for s1 in (0, 3, 1, 2):
        by = (y + jnp.where(lead, s3, s1)) % 4
        bx = (x + jnp.where(lead, s1, s3)) % 4
        blk = ((z + 4 - by) % 4) * 4 + bx
        parts.append(jnp.concatenate([own[blk], oth[blk]], 0))
    return jnp.concatenate(parts, 1)


def project_early_kernel(own, oth, *refs):
    pieces = refs[:9]
    acc, wall, sems = refs[9:]
    copies = save_pieces(pieces, EARLY, wall, 0, sems)
    for n, group in enumerate(((0, 1, 2), (3, 5, 7), (4, 6, 8))):
        lhs = group_lhs(own, oth, (0, 3, 1)[n])
        for j in range(3):
            cols = slice(j * 256, (j + 1) * 256)
            r = dot_nn(lhs, rows_of([pieces[at] for at in group], j))
            if n == 0:
                acc[:, cols] = r
            else:
                acc[:, cols] += r
    for copy in copies:
        copy.wait()


def project_late_kernel(own, oth, acc, wall_in, *refs):
    pieces = refs[:6]
    proj, agg, wall, sems = refs[6:]
    copies = save_pieces(pieces, LATE, wall, 12, sems)
    lhs = group_lhs(own, oth, 2)
    for j in range(3):
        cols = slice(j * 256, (j + 1) * 256)
        r = dot_nn(lhs, rows_of(pieces, j))
        proj[:, cols] = (acc[:, cols] + r).astype(BF)
    mask = same_patch(128, 128)
    where = [(g, h) for g in range(2) for h in range(2)]
    firsts = first_step(proj, where, mask)
    for (g, h), f in zip(where, firsts):
        m = jnp.sum(f.reshape(CHG, PAT, HD), axis=0) * (1.0 / CHG)
        agg[:, h, pl.ds(g * PAT, PAT), :] = jnp.broadcast_to(m.astype(BF)[None], (16, PAT, HD))
    for copy in copies:
        copy.wait()


def first_step(proj, where, mask):
    def part(g, h, j):
        return proj[pl.ds(g * 128, 128), pl.ds(j * 256 + h * 128, 128)]

    qs = [part(g, h, 0) for g, h in where]
    ks = [part(g, h, 1).astype(F32) for g, h in where]
    kns = [(k * inv_norm(k)).astype(BF) for k in ks]
    rqs = [inv_norm(q.astype(F32)) * FAC for q in qs]
    scores = [dot_nt(q, kn) * rq for q, kn, rq in zip(qs, kns, rqs)]
    ws = [softmax_rows(sc, mask).astype(BF) for sc in scores]
    return [dot_nn(w, part(g, h, 2)) for w, (g, h) in zip(ws, where)]


def across_kernel(proj, agg, mix_own, mix_oth, soft):
    mask = same_patch(256, 256)
    small = same_patch(128, 128)
    where = [(g, h) for h in range(2) for g in range(2)]
    seconds = []
    for h in range(2):
        q = proj[:, pl.ds(h * 128, 128)]
        rq = inv_norm(q.astype(F32))
        a = agg[:, h].reshape(256, HD)
        af = a.astype(F32)
        an = (af * inv_norm(af)).astype(BF)
        w = softmax_rows(dot_nt(q, an) * (rq * FAC), mask)
        soft[h] = w
        seconds.append(dot_nn(w.astype(BF), a))
    firsts = first_step(proj, where, small)
    for (g, h), first in zip(where, firsts):
        ref = (mix_own, mix_oth)[g]
        ref[:, pl.ds(h * 128, 128)] = (first + seconds[h][g * 128:(g + 1) * 128]).astype(BF)


def across_back_kernel(proj, agg, gm_mine, gm_got, soft, gg, gagg):
    for h in range(2):
        cols = pl.ds(h * 128, 128)
        qf = proj[:, cols].astype(F32)
        rq = inv_norm(qf)
        a = agg[:, h].reshape(256, HD)
        af = a.astype(F32)
        ra = inv_norm(af)
        an = (af * ra).astype(BF)
        w = soft[h]
        wb = w.astype(BF)
        gf = jnp.concatenate([gm_mine[:, cols], gm_got[:, cols]], 0)
        g = gf.astype(BF)
        dw = dot_nt(g, a)
        wdw = w * dw
        dsb = ((wdw - w * jnp.sum(wdw, axis=-1, keepdims=True)) * FAC).astype(BF)
        gg[:, cols] = gf
        gg[:, pl.ds(256 + h * 128, 128)] = norm_back(qf, rq, dot_nn(dsb, an))
        dan = dot_tn(dsb, (qf * rq).astype(BF))
        da = dot_tn(wb, g) + norm_back(af, ra, dan)
        gagg[:, h] = da.astype(BF).reshape(16, 16, HD)


def quarter_slots(d):
    y, x, core, z = place()
    by = (z + d) % 4
    py = slot_of((by + 4 - y) % 4)
    slots = []
    for bx in range(4):
        px = slot_of((bx + 4 - x) % 4)
        slots.append(jnp.where(core == 0, py * 4 + px, px * 4 + py))
    return slots


def fetch(wall, wv, sems, d, at):
    copies = []
    for bx, slot in enumerate(quarter_slots(d)):
        copy = pltpu.make_async_copy(wall.at[slot], wv.at[at + bx], sems.at[at + bx])
        copy.start()
        copies.append(copy)
    return copies


def block_product(stk, wv, n):
    w = jnp.concatenate([wv[n, :, j].reshape(256, 256) for j in range(3)], 1)
    return dot_nt(stk[...], w)


def back_kernel(proj, gg, ragg, wall, own, oth, stk, corr_own, corr_oth, wv, sems):
    copies = fetch(wall, wv, sems, 2, 0)
    own_grad = jnp.sum(ragg[...].astype(F32), axis=0) * (1.0 / CHG)
    mask = same_patch(128, 128)
    where = [(g, h) for g in range(2) for h in range(2)]
    fwd = [within(proj, pl.ds(g * 128, 128), h, mask) for g, h in where]
    grads = []
    for g, h in where:
        og = own_grad[h, g * PAT:(g + 1) * PAT, :]
        gf = gg[pl.ds(g * 128, 128), pl.ds(h * 128, 128)]
        grads.append((gf + jnp.broadcast_to(og[None], (CHG, PAT, HD)).reshape(128, HD)).astype(BF))
    dws = [dot_nt(gb, f[2]) for gb, f in zip(grads, fwd)]
    dvs = [dot_tn(f[6].astype(BF), gb).astype(BF) for gb, f in zip(grads, fwd)]
    dss = []
    for f, dw in zip(fwd, dws):
        wdw = f[6] * dw
        dss.append(((wdw - f[6] * jnp.sum(wdw, axis=-1, keepdims=True)) * FAC).astype(BF))
    dqs = [dot_nn(ds, f[5]) for ds, f in zip(dss, fwd)]
    dks = [dot_tn(ds, (f[0] * f[3]).astype(BF)) for ds, f in zip(dss, fwd)]
    totals = [jnp.zeros((128, 1), F32), jnp.zeros((128, 1), F32)]
    for n, (g, h) in enumerate(where):
        qf, kf, v, rq, rk, _, _ = fwd[n]
        rows = pl.ds(g * 128, 128)
        dq = (norm_back(qf, rq, dqs[n]) + gg[rows, pl.ds(256 + h * 128, 128)]).astype(BF)
        dk = norm_back(kf, rk, dks[n]).astype(BF)
        stk[rows, pl.ds(h * 128, 128)] = dq
        stk[rows, pl.ds(256 + h * 128, 128)] = dk
        stk[rows, pl.ds(512 + h * 128, 128)] = dvs[n]
        prod = dq.astype(F32) * qf + dk.astype(F32) * kf + dvs[n].astype(F32) * v.astype(F32)
        totals[g] = totals[g] + jnp.sum(prod, axis=-1, keepdims=True)
    corr_own[...] = jnp.broadcast_to(totals[0], (128, 128))
    corr_oth[...] = jnp.broadcast_to(totals[1], (128, 128))
    for copy in copies:
        copy.wait()

    def step(bx, carry):
        r = block_product(stk, wv, bx)
        cols = pl.ds(pl.multiple_of(bx * 256, 256), 256)
        own[:, cols] = r[0:128].astype(BF)
        oth[:, cols] = r[128:256].astype(BF)
        return carry

    lax.fori_loop(0, 4, step, 0)


def side_kernel(stk, wall, own, oth, wv, sems):
    copies = []
    for n, d in enumerate((1, 3)):
        copies.append(fetch(wall, wv, sems, d, n * 4))
    for n in range(2):
        for copy in copies[n]:
            copy.wait()

        def step(bx, carry):
            r = block_product(stk, wv, n * 4 + bx)
            cols = pl.ds(pl.multiple_of(bx * 256, 256), 256)
            own[n, :, cols] = r[0:128].astype(BF)
            oth[n, :, cols] = r[128:256].astype(BF)
            return carry

        lax.fori_loop(0, 4, step, 0)


def home_kernel(stk, wall, own, oth, wv, sems):
    for copy in fetch(wall, wv, sems, 0, 0):
        copy.wait()

    def step(bx, carry):
        r = block_product(stk, wv, bx)
        cols = pl.ds(pl.multiple_of(bx * 256, 256), 256)
        own[:, cols] = r[0:128].astype(BF)
        oth[:, cols] = r[128:256].astype(BF)
        return carry

    lax.fori_loop(0, 4, step, 0)


def combine(mine, got, part, inv, corr_own, corr_got):
    r = inv[:, 0:1]
    c = (corr_own[:, 0:1] + corr_got[:, 0:1]) * (r * (1.0 / 4096))
    h = part[0:128, :].astype(F32)
    g = part[128:136, :].astype(F32)[0:1]
    return r * (g * (mine.astype(F32) + got.astype(F32)) - h * c)


def one_kernel(mine, got, part, inv, corr_own, corr_got, out):
    out[...] = combine(mine[...], got[...], part, inv, corr_own, corr_got).astype(BF)


def two_kernel(mine, got, part_a, part_b, inv, corr_own, corr_got, out_a, out_b):
    out_a[...] = combine(mine[0], got[0], part_a, inv, corr_own, corr_got).astype(BF)
    out_b[...] = combine(mine[1], got[1], part_b, inv, corr_own, corr_got).astype(BF)


def last_kernel(mine, got, part, inv, corr_own, corr_got, cot, r1, r2, r3, out):
    grad = combine(mine[...], got[...], part, inv, corr_own, corr_got)
    grad = grad + r1[...].astype(F32) + r2[...].astype(F32) + r3[...].astype(F32)
    out[...] = (cot[...].astype(F32) + grad).astype(BF)


def gm_kernel(c0, c1, c2, c3, ow, mine, other):
    _, _, core, z = place()
    for ref, which in ((mine, core), (other, 1 - core)):
        rows = pl.ds(pl.multiple_of(which * 256, 256), 256)
        total = jnp.zeros((128, 256), F32)
        for d, c in enumerate((c0, c1, c2, c3)):
            cols = pl.ds(pl.multiple_of(((z + 4 - d) % 4) * 1024, 1024), 1024)
            total = total + dot_nt(c[...], ow[rows, cols])
        ref[...] = total


def out_quarter(mine, got, ow, d):
    _, _, core, z = place()
    cols = pl.ds(pl.multiple_of(((z + d) % 4) * 1024, 1024), 1024)
    rows = pl.ds(pl.multiple_of(core * 256, 256), 256)
    rows_got = pl.ds(pl.multiple_of((1 - core) * 256, 256), 256)
    return dot_nn(mine[...], ow[rows, cols]) + dot_nn(got[...], ow[rows_got, cols])


def out_first_kernel(mine, got, ow, o2):
    o2[...] = out_quarter(mine, got, ow, 2).astype(BF)


def out_rest_kernel(mine, got, ow, o1, o3, o0):
    o1[...] = out_quarter(mine, got, ow, 1).astype(BF)
    o3[...] = out_quarter(mine, got, ow, 3).astype(BF)
    o0[...] = out_quarter(mine, got, ow, 0)


VM = pl.BlockSpec(memory_space=pltpu.VMEM)
AN = pl.BlockSpec(memory_space=pl.ANY)
HB = pl.BlockSpec(memory_space=pltpu.HBM)
PARAMS = pltpu.CompilerParams(vmem_limit_bytes=16 * 1024 * 1024)


def shape(dims, dtype):
    return jax.ShapeDtypeStruct(dims, dtype)


def call(kernel, ins, outs, args, scratch=()):
    return pl.pallas_call(
        kernel,
        in_specs=ins,
        out_specs=[spec for spec, _ in outs],
        out_shape=[sh for _, sh in outs],
        scratch_shapes=list(scratch),
        compiler_params=PARAMS,
    )(*args)


BLOCK = (2, 3, 128, 256)


def in_hbm(value):
    return pltpu.with_memory_space_constraint(value, pltpu.HBM)


def prepare(tokens, position, gain):
    return call(
        prepare_kernel, [HB] * 3, [(VM, shape((136, 1024), BF))],
        (in_hbm(tokens), in_hbm(position), in_hbm(gain)),
        (
            pltpu.VMEM((16, 8, 1024), BF), pltpu.VMEM((16, 1024), BF), pltpu.VMEM((1024,), BF),
            pltpu.SemaphoreType.DMA((3,)),
        ),
    )[0]


def normalise(parts):
    return call(
        norm_kernel, [VM] * 4,
        [(VM, shape((16, 128, 256), BF)), (VM, shape((128, 128), F32))], parts,
    )


WALL = pltpu.HBM((16,) + BLOCK, BF)


def project_early(own, oth, weights):
    return call(
        project_early_kernel, [VM, VM] + [VM] * 9,
        [(VM, shape((256, 768), F32)), (HB, WALL)],
        (own, oth) + weights,
        (pltpu.SemaphoreType.DMA((9,)),),
    )


def project_late(own, oth, acc, wall, weights):
    return pl.pallas_call(
        project_late_kernel,
        in_specs=[VM, VM, VM, HB] + [VM] * 6,
        out_specs=[VM, VM, HB],
        out_shape=[shape((256, 768), BF), shape((16, 2, 16, HD), BF), WALL],
        scratch_shapes=[pltpu.SemaphoreType.DMA((6,))],
        input_output_aliases={3: 2},
        compiler_params=PARAMS,
        name="late",
    )(own, oth, acc, in_hbm(wall), *weights)


def across(proj, agg):
    return call(
        across_kernel, [VM] * 2,
        [(VM, shape((128, 256), BF)), (VM, shape((128, 256), BF)), (VM, shape((2, 256, 256), F32))],
        (proj, agg),
    )


def across_back(proj, agg, gm_mine, gm_got, soft):
    return call(
        across_back_kernel, [VM] * 5,
        [(VM, shape((256, 512), F32)), (VM, shape((16, 2, 16, HD), BF))],
        (proj, agg, gm_mine, gm_got, soft),
    )


def backward(proj, gg, ragg, wall):
    return call(
        back_kernel, [VM] * 3 + [HB],
        [
            (VM, shape((128, 1024), BF)), (VM, shape((128, 1024), BF)), (VM, shape((256, 768), BF)),
            (VM, shape((128, 128), F32)), (VM, shape((128, 128), F32)),
        ],
        (proj, gg, ragg, in_hbm(wall)),
        (pltpu.VMEM((4,) + BLOCK, BF), pltpu.SemaphoreType.DMA((4,))),
    )


def side(stk, wall):
    return call(
        side_kernel, [VM, HB], [(VM, shape((2, 128, 1024), BF))] * 2, (stk, in_hbm(wall)),
        (pltpu.VMEM((8,) + BLOCK, BF), pltpu.SemaphoreType.DMA((8,))),
    )


def home(stk, wall):
    return call(
        home_kernel, [VM, HB], [(VM, shape((128, 1024), BF))] * 2, (stk, in_hbm(wall)),
        (pltpu.VMEM((4,) + BLOCK, BF), pltpu.SemaphoreType.DMA((4,))),
    )


def own_weights(qkv_weight, core):
    mine = lax.dynamic_slice_in_dim(qkv_weight, core * 256, 256, 2)
    other = lax.dynamic_slice_in_dim(qkv_weight, (1 - core) * 256, 256, 2)
    got = swap(other)
    lead = core == 0
    return jnp.stack([jnp.where(lead, mine, got), jnp.where(lead, got, mine)])


def gather_weights(own):
    def near(value, step):
        return lax.ppermute(value, "chan", ring(True, step))

    def cross(value, step):
        return lax.ppermute(value, "chan", ring(False, step))

    r = near(own, 1)
    l = near(own, -1)

    up = cross(own, 1)
    down = cross(own, -1)
    pair = jnp.stack([r, l])
    far = jnp.concatenate([near(r[:1], 1), near(l[1:], -1)], 0)
    pair_up = cross(pair, 1)
    pair_down = cross(pair, -1)
    over_a = cross(up[:1], 1)
    over_b = cross(down[1:], -1)
    far_up = cross(far, 1)
    far_down = cross(far, -1)
    pair_a = cross(pair_up[0], 1)
    pair_b = cross(pair_down[1], -1)
    far_up_half = far_up[:1]
    far_down_half = far_down[1:]
    far_a = cross(far_up_half, 1)
    far_b = cross(far_down_half, -1)

    def whole(value):
        return value.reshape((-1,) + value.shape[-4:])

    lead = tuple(whole(v) for v in (own, pair, far, up, down, pair_up, pair_down, far_up, far_down))
    tail = (over_a, over_b, whole(pair_a), whole(pair_b), far_a, far_b)
    return lead, tail, far


def layer(tokens, position, gain, qkv_weight, out_weight, cotangent):
    _, _, core, _ = place()

    own_w = own_weights(qkv_weight, core)
    message = prepare(tokens, position, gain)
    h_parts = [message]
    for d in (1, 2, 3):
        h_parts.append(zshift(message, d))
    early, late, far = gather_weights(own_w)

    waited, _ = lax.optimization_barrier((h_parts, far))
    normed, inv_rms = normalise(waited)
    cot = cotangent.reshape(128, 1024)
    c_parts = [cot]
    for d in (1, 2, 3):
        c_parts.append(zshift(cot, d))
    normed_other = swap(normed)
    acc, wall = project_early(normed, normed_other, early)
    proj, agg, wall = project_late(normed, normed_other, acc, wall, late)
    agg_all = lax.all_to_all(agg, "chan", 0, 0, axis_index_groups=SAME_CORE, tiled=True)

    gm_mine, gm_other = call(
        gm_kernel, [VM] * 5, [(VM, shape((128, 256), F32))] * 2, c_parts + [out_weight],
    )
    gm_got = swap(gm_other)

    mix_own, mix_oth, soft = across(proj, agg_all)
    mix_got = swap(mix_oth)
    gg, gagg = across_back(proj, agg_all, gm_mine, gm_got, soft)
    ragg = lax.all_to_all(gagg, "chan", 0, 0, axis_index_groups=SAME_CORE, tiled=True)

    o2, = call(
        out_first_kernel, [VM] * 3, [(VM, shape((128, 1024), BF))], (mix_own, mix_got, out_weight),
    )
    s2 = zshift(o2, 2)
    o1, o3, o0 = call(
        out_rest_kernel, [VM] * 3,
        [(VM, shape((128, 1024), BF)), (VM, shape((128, 1024), BF)), (VM, shape((128, 1024), F32))],
        (mix_own, mix_got, out_weight),
    )
    s1 = zshift(o1, 1)
    s3 = zshift(o3, 3)
    summed = o0 + s1.astype(F32) + s2.astype(F32) + s3.astype(F32)
    layer_out = (summed + message[:128].astype(F32)).astype(BF)

    own2, oth2, stk, corr_own, corr_oth = backward(proj, gg, ragg, wall)
    got2 = swap(oth2)
    corr_got = swap(corr_oth)
    own_r, oth_r = side(stk, wall)
    got_r = swap(oth_r)
    scal = (inv_rms, corr_own, corr_got)
    msg2, = call(one_kernel, [VM] * 6, [(VM, shape((128, 1024), BF))], (own2, got2, h_parts[2]) + scal)
    r2 = zshift(msg2, 2)
    msg1, msg3 = call(
        two_kernel, [VM] * 7, [(VM, shape((128, 1024), BF))] * 2,
        (own_r, got_r, h_parts[3], h_parts[1]) + scal,
    )
    r1 = zshift(msg1, 1)
    r3 = zshift(msg3, 3)
    own_h, oth_h = home(stk, wall)
    got_h = swap(oth_h)
    input_grad, = call(
        last_kernel, [VM] * 10, [(VM, shape((128, 1024), BF))],
        (own_h, got_h, h_parts[0]) + scal + (cot, r1, r2, r3),
    )
    return layer_out.reshape(16, 8, 1024), input_grad.reshape(16, 8, 1024)


def solution(mesh):
    return jax.shard_map(
        layer,
        mesh=mesh,
        in_specs=(
            P("chan", "region", "head"),
            P("chan", "head"),
            P("head"),
            P(None, "chan", "head"),
            P("head", None),
            P("chan", "region", "head"),
        ),
        out_specs=(P("chan", "region", "head"), P("chan", "region", "head")),
        check_vma=False,
    )
```
